128 devices in a mesh: row: 16 (over x_lo, y, core), col: 8 (over z, x_hi).
Axes of the slice: x: 4 (x_hi: 2, x_lo: 2; x = x_hi * 2 + x_lo), y: 4, z: 4, core: 2. Of those that a mesh axis runs over, the one named last changes fastest.
Arguments:
- surface_height: float32 [2048, 2048], P('row', 'col'), may hold values from -1.2 to 1.2
- surface_potential: float32 [2048, 2048], P('row', 'col'), may hold values from -4 to 4
- velocity: float32 [3, 16, 1024, 1024], P(None, None, 'row', 'col'), may hold values from -1.25 to 1.25
Outputs:
- height_rate: float32 [2048, 2048], P('row', 'col')
- potential_rate: float32 [2048, 2048], P('row', 'col')
- velocity_next: float32 [3, 16, 1024, 1024], P(None, None, 'row', 'col')
The draws below stay inside these ranges and needn't reach their ends.
All inputs are finite; a program needn't handle non-finite values.
Results may differ from the reference program's by a relative error of at most 0.00019.
Values sent between devices are 32-bit elements; how exact they have to be, the bound alone decides.
A program may use at most 128 MiB of HBM per device.

```python
import jax
import jax.numpy as jnp

NX = 2048
NY = 2048
LZ = 16
COARSE = 2
LYALL = 1024
LXALL = 1024


def draw_surface_height(key, part):
    rough_key = jax.random.fold_in(jax.random.fold_in(key, 11), 0)
    return 0.3 * jnp.clip(jax.random.normal(rough_key, (NY, NX), jnp.float32), -4.0, 4.0)


def draw_surface_potential(key, part):
    rough_key = jax.random.fold_in(jax.random.fold_in(key, 23), 0)
    return jnp.clip(jax.random.normal(rough_key, (NY, NX), jnp.float32), -4.0, 4.0)


def block_levels(rng, dims, cuts, smallest, largest):
    def one(axis_at, parts):
        draws = jax.random.uniform(jax.random.fold_in(jax.random.fold_in(rng, 6), axis_at), (parts,), jnp.float32, smallest / len(cuts), largest / len(cuts))
        return jnp.repeat(jnp.exp(draws), dims[axis_at] // parts).reshape((-1,) + (1,) * (len(dims) - axis_at - 1))

    level = one(*cuts[0])
    for cut in cuts[1:]:
        level = level * one(*cut)
    return level


def noise(own_key, shape, deviation, limit, cuts=(), held_as=jnp.bfloat16):
    array = jax.random.normal(own_key, shape, jnp.float32) * deviation
    if len(cuts) > 0:
        array = block_levels(own_key, shape, cuts, -0.22, 0.18) * array
    return jnp.clip(array, min=-limit, max=limit).astype(held_as)


def setup_inputs(seed: int = 0) -> dict:
    arg_keys = jax.random.split(jax.random.key(seed), 4)
    return {
        "surface_height": draw_surface_height(jax.random.fold_in(arg_keys[3], 71), 0),
        "surface_potential": draw_surface_potential(jax.random.fold_in(arg_keys[3], 71), 0),
        "velocity": noise(arg_keys[2], (3, LZ, LYALL, LXALL), 0.2, 1.25, ((2, 16), (3, 8)), jnp.float32),
    }


GRAVITY = 1.0
SURFACE_STEP = 0.05
FLOW_STEP = 0.5
VISCOSITY = 0.2
DECAY_RATE = 0.05

def wave_numbers(index, length):
    signed = jnp.where(index < length // 2, index, index - length)
    kept_mask = (jnp.abs(signed) <= length // 3).astype(jnp.float32)
    return (2.0 * jnp.pi / length * signed.astype(jnp.float32), kept_mask)

def coarsen(source):
    rows_out = source.shape[0] // COARSE
    cols_out = source.shape[1] // COARSE
    return source.reshape(rows_out, COARSE, cols_out, COARSE).mean(axis=(1, 3))

def flow_update(padded_flow, padded_load, surface_u, surface_v):
    depth_count = padded_flow.shape[1]
    level_mid = jnp.arange(depth_count, dtype=jnp.float32)[:, None, None] + 0.5
    drift_decay = jnp.exp(-2.0 * DECAY_RATE * level_mid)
    load_decay = jnp.exp(-DECAY_RATE * level_mid)

    def derivs(source, top_value):
        middle = source[:, 1:-1, 1:-1]
        above_cell = jnp.concatenate([top_value[None], middle[:-1]], axis=0)
        below_cell = jnp.concatenate([middle[1:], middle[-1:]], axis=0)
        east_side = source[:, 1:-1, 2:]
        west_side = source[:, 1:-1, :-2]
        north_side = source[:, 2:, 1:-1]
        south_side = source[:, :-2, 1:-1]
        laplace = east_side + west_side + north_side + south_side + above_cell + below_cell - 6.0 * middle
        return (middle, 0.5 * (east_side - west_side), 0.5 * (north_side - south_side), 0.5 * (above_cell - below_cell), laplace)
    u_mid, u_dx, u_dy, u_dz, u_lap = derivs(padded_flow[0], surface_u)
    v_mid, v_dx, v_dy, v_dz, v_lap = derivs(padded_flow[1], surface_v)
    w_mid, w_dx, w_dy, w_dz, w_lap = derivs(padded_flow[2], jnp.zeros_like(surface_u))
    vort_x = w_dy - v_dz
    vort_y = u_dz - w_dx
    vort_z = v_dx - u_dy
    drift_u = surface_u[None] * drift_decay
    drift_v = surface_v[None] * drift_decay
    load_x = 0.5 * (padded_load[1:-1, 2:] - padded_load[1:-1, :-2])[None] * load_decay
    load_y = 0.5 * (padded_load[2:, 1:-1] - padded_load[:-2, 1:-1])[None] * load_decay

    def advance(middle, slope_x, slope_y, slope_z, laplace, forcing):
        carried = u_mid * slope_x + v_mid * slope_y + w_mid * slope_z
        return middle + FLOW_STEP * (-carried + VISCOSITY * laplace + forcing)
    next_u = advance(u_mid, u_dx, u_dy, u_dz, u_lap, drift_v * vort_z - load_x)
    next_v = advance(v_mid, v_dx, v_dy, v_dz, v_lap, -drift_u * vort_z - load_y)
    next_w = advance(w_mid, w_dx, w_dy, w_dz, w_lap, drift_u * vort_y - drift_v * vort_x)
    return jnp.stack([next_u, next_v, next_w])

def reference(surface_height, surface_potential, velocity):
    kx_values, kx_kept = wave_numbers(jnp.arange(NX, dtype=jnp.int32), NX)
    ky_values, ky_kept = wave_numbers(jnp.arange(NY, dtype=jnp.int32), NY)
    kx_grid = kx_values[None, :]
    ky_grid = ky_values[:, None]
    mask = ky_kept[:, None] * kx_kept[None, :]
    magnitude = jnp.sqrt(kx_grid * kx_grid + ky_grid * ky_grid)

    def forward(source):
        return jnp.fft.fft2(source) * mask

    def backward(spectrum, factor):
        return jnp.real(jnp.fft.ifft2(spectrum * factor))
    height = surface_height
    pot_hat = forward(surface_potential)
    height_hat = forward(height)
    vert_one = backward(pot_hat, magnitude)
    curve_one = backward(pot_hat, magnitude * magnitude)
    cube_one = backward(pot_hat, magnitude * magnitude * magnitude)
    pot_dx = backward(pot_hat, 1j * kx_grid)
    pot_dy = backward(pot_hat, 1j * ky_grid)
    height_dx = backward(height_hat, 1j * kx_grid)
    height_dy = backward(height_hat, 1j * ky_grid)
    second_pot = -height * vert_one
    second_hat = forward(second_pot)
    vert_two = backward(second_hat, magnitude)
    curve_two = backward(second_hat, magnitude * magnitude)
    third_pot = -height * vert_two - 0.5 * height * height * curve_one
    vert_three = backward(forward(third_pot), magnitude)
    vertical = vert_one + vert_two + vert_three + height * (curve_one + curve_two) + 0.5 * height * height * cube_one
    slope = height_dx * height_dx + height_dy * height_dy
    height_rate = -(height_dx * pot_dx + height_dy * pot_dy) + (1.0 + slope) * vertical
    potential_rate = -GRAVITY * height - 0.5 * (pot_dx * pot_dx + pot_dy * pot_dy) + 0.5 * (1.0 + slope) * vertical * vertical
    pressure = GRAVITY * coarsen(height + SURFACE_STEP * height_rate)
    surface_u = coarsen(pot_dx)
    surface_v = coarsen(pot_dy)
    padded_flow = jnp.pad(velocity, ((0, 0), (0, 0), (1, 1), (1, 1)), mode='wrap')
    padded_load = jnp.pad(pressure, ((1, 1), (1, 1)), mode='wrap')
    velocity_next = flow_update(padded_flow, padded_load, surface_u, surface_v)
    return (height_rate, potential_rate, velocity_next)
```

```python
import functools

import jax
import jax.numpy as jnp
import numpy as np
from jax import lax
from jax.experimental import pallas as pl
from jax.experimental.pallas import tpu as pltpu
from jax.sharding import PartitionSpec as P

N = 2048
KEPT = N // 3
ROWS = 16
COLS = 8
DEVS = ROWS * COLS
LINES = 16
OWNERS = 86
OWN_PAD = 88
LANES = 128
LZ = 16
GRAVITY = 1.0
SURFACE_STEP = 0.05
FLOW_STEP = 0.5
VISCOSITY = 0.2
DECAY_RATE = 0.05
MESH = pl.DeviceIdType.MESH
F32 = jnp.float32
BF16 = jnp.bfloat16
VMEM = pltpu.VMEM


def block_complex(c, s):
    return np.block([[c, -s], [s, c]])


def split_table(t):
    hi = t.astype(np.float32).astype(jnp.bfloat16)
    lo = (t - hi.astype(np.float64)).astype(np.float32).astype(jnp.bfloat16)
    return hi, lo


@functools.cache
def tables():
    def wave(a, b, n):
        ang = 2.0 * np.pi * ((a[:, None] * b[None, :]) % n) / n
        return np.cos(ang), np.sin(ang)

    r8, r16, r128, r256 = (np.arange(k) for k in (8, 16, 128, 256))
    own = np.arange(OWN_PAD)
    eye16, eye8 = np.eye(16), np.eye(8)
    c8, s8 = wave(r8, r8, 8)
    c16, s16 = wave(r16, r16, 16)
    x_first = np.concatenate([np.kron(c8, eye16), np.kron(-s8, eye16)], axis=1)
    x_last = np.concatenate([np.kron(c8, eye16), np.kron(-s8, eye16)], axis=0)
    cp, sp = wave(own, r256, 256)
    x_second = block_complex(cp, -sp)
    x_third = block_complex(cp.T, sp.T)
    c1, s1 = wave(r128, r128, 128)
    y_first = block_complex(c1, -s1)
    y_last = block_complex(c1, s1)
    y_second = block_complex(np.kron(eye8, c16), np.kron(eye8, s16))
    y_third = block_complex(np.kron(eye8, c16), np.kron(eye8, -s16))
    ct, st = wave(r256, r8, N)
    x_twist = np.stack([np.repeat(ct, 16, axis=1), np.repeat(st, 16, axis=1)])
    ct, st = wave(r128, r16, N)
    y_twist = np.stack([np.tile(ct, (1, 8)), np.tile(st, (1, 8))])
    pairs = np.kron(np.eye(128), np.ones((2, 1))) * 0.25
    mats = [x_first, x_second, x_third, x_last, y_first, y_second, y_third, y_last]
    out = []
    for m in mats:
        out.extend(split_table(m))
    out.append(pairs.astype(np.float32).astype(jnp.bfloat16))
    out.append(x_twist.astype(np.float32))
    out.append(y_twist.astype(np.float32))
    return tuple(out)


def split(a):
    hi = a.astype(BF16)
    return hi, (a - hi.astype(F32)).astype(BF16)


def dot(a, b):
    return lax.dot_general(a, b, (((1,), (0,)), ((), ())), preferred_element_type=F32)


def left_table(table, data):
    th, tl = table
    dh, dl = split(data)
    return dot(th, dh) + dot(th, dl) + dot(tl, dh)


def right_table(data, table):
    th, tl = table
    dh, dl = split(data)
    return dot(dh, th) + dot(dl, th) + dot(dh, tl)


def x_forward(phys, first, second, twist):
    z = right_table(phys, first)
    zr, zi = z[:, :LANES], z[:, LANES:]
    c, s = twist
    t = jnp.concatenate([zr * c + zi * s, zi * c - zr * s], axis=0)
    out = left_table(second, t)
    return out[:OWN_PAD], out[OWN_PAD:]


def x_inverse(re, im, third, last, twist):
    u = left_table(third, jnp.concatenate([re, im], axis=0))
    ur, ui = u[:256], u[256:]
    c, s = twist
    t = jnp.concatenate([ur * c - ui * s, ur * s + ui * c], axis=1)
    return right_table(t, last)


def y_forward(re, im, first, second, twist):
    t = left_table(first, jnp.concatenate([re, im], axis=0))
    tr, ti = t[:LANES], t[LANES:]
    c, s = twist
    z = right_table(jnp.concatenate([tr * c + ti * s, ti * c - tr * s], axis=1), second)
    return z[:, :LANES], z[:, LANES:]


def y_inverse(re, im, third, last, twist):
    u = right_table(jnp.concatenate([re, im], axis=1), third)
    ur, ui = u[:, :LANES], u[:, LANES:]
    c, s = twist
    out = left_table(last, jnp.concatenate([ur * c - ui * s, ur * s + ui * c], axis=0))
    return out[:LANES], out[LANES:]


def wave_grids(p):
    lane = lax.broadcasted_iota(jnp.int32, (LANES, LANES), 1)
    q1 = lax.broadcasted_iota(jnp.int32, (LANES, LANES), 0)
    kx_index = lane // 16 + 8 * p
    ky_index = q1 + 128 * (lane % 16)
    ky_signed = jnp.where(ky_index < N // 2, ky_index, ky_index - N)
    unit = np.float32(2.0 * np.pi / N)
    kx = unit * kx_index.astype(F32)
    ky = unit * ky_signed.astype(F32)
    kept = (jnp.abs(ky_signed) <= KEPT) & (kx_index <= KEPT)
    fold = jnp.where(kx_index == 0, 1.0, 2.0) / float(N * N)
    weight = jnp.where(kept, fold, 0.0).astype(F32)
    return kx, ky, jnp.sqrt(kx * kx + ky * ky), weight


def owner_place(p):
    late = (p >= 64).astype(jnp.int32)
    chip = p + late * (2 * p - 192)
    return 2 * (chip // COLS) + late, chip % COLS


def get(buf, j, count):
    return buf[:count, j, :]


def put(buf, j, value):
    buf[: value.shape[0], j, :] = value


def surface_kernel(*refs):
    phi_ref, eta_ref, vel_ref = refs[:3]
    n_tab = 19
    tab = refs[3 : 3 + n_tab]
    outs = refs[3 + n_tab : 3 + n_tab + 10]
    (height_out, pot_out, su_out, sv_out, lx_out, press_out, low_y, high_y, low_x, high_x) = outs
    (
        lines,
        fields,
        send1,
        recv1,
        send2,
        recv2,
        send2b,
        recv2b,
        send3,
        recv3,
        send4,
        recv4,
        send5,
        recv5,
        send6,
        recv6,
        spec,
        turned,
        out_t,
        coarse_t,
        vel,
        pack_y,
        pack_x,
        vel_sem,
        send_sems,
        recv_sems,
        out_sems,
        halo_sems,
    ) = refs[3 + n_tab + 10 :]
    row, col = lax.axis_index("row"), lax.axis_index("col")
    me = row * COLS + col
    chip = (row // 2) * COLS + col
    core = row % 2
    is_owner = (core == 0) | (chip % 3 == 0)
    my_p = jnp.where(core == 0, chip, 64 + chip // 3)

    def tables_at(k):
        return tab[2 * k][...], tab[2 * k + 1][...]

    pairs_ref, x_twist_ref, y_twist_ref = tab[16:19]

    def remote(src, dst, send_sem, recv_sem, place):
        return pltpu.make_async_remote_copy(
            src_ref=src,
            dst_ref=dst,
            send_sem=send_sem,
            recv_sem=recv_sem,
            device_id=place,
            device_id_type=MESH,
        )

    def wait_bytes(ref, sem):
        pltpu.make_async_copy(ref, ref, sem).wait()

    vel_copy = pltpu.make_async_copy(vel_ref, vel, vel_sem)
    vel_copy.start()

    barrier = pltpu.get_barrier_semaphore()

    def greet(i, _):
        other = lax.rem(me + i, DEVS)
        pl.semaphore_signal(barrier, inc=1, device_id=(other // COLS, other % COLS), device_id_type=MESH)
        return 0

    lax.fori_loop(1, DEVS, greet, 0)
    for buf in (recv2, recv2b, recv4, recv6):
        buf[OWNERS:OWN_PAD] = jnp.zeros((OWN_PAD - OWNERS,) + buf.shape[1:], F32)
    pl.semaphore_wait(barrier, DEVS - 1)

    for f, ref in enumerate((phi_ref, eta_ref)):
        for i in range(1, COLS):
            to = lax.rem(col + i, COLS)
            remote(
                ref.at[pl.ds(to * LINES, LINES), :],
                lines.at[f, col],
                send_sems.at[f],
                recv_sems.at[f],
                (row, to),
            ).start()
        pltpu.make_async_copy(
            ref.at[pl.ds(col * LINES, LINES), :], lines.at[f, col], recv_sems.at[f]
        ).start()

    def to_owners(send, recv, k):
        def step(i, _):
            p = lax.rem(me + i, OWNERS)
            r, c = owner_place(p)

            @pl.when(r * COLS + c != me)
            def _():
                remote(send.at[p], recv.at[me], send_sems.at[k], recv_sems.at[k], (r, c)).start()

            @pl.when(r * COLS + c == me)
            def _():
                pltpu.make_async_copy(send.at[p], recv.at[me], recv_sems.at[k]).start()

            return 0

        lax.fori_loop(0, OWNERS, step, 0)

    def to_lines(send, recv, k):
        def step(i, _):
            other = lax.rem(me + i, DEVS)
            remote(
                send.at[other],
                recv.at[my_p],
                send_sems.at[k],
                recv_sems.at[k],
                (other // COLS, other % COLS),
            ).start()
            return 0

        lax.fori_loop(1, DEVS, step, 0)
        pltpu.make_async_copy(send.at[me], recv.at[my_p], recv_sems.at[k]).start()

    def forward_x(f, send, j):
        re, im = x_forward(fields[f], tables_at(0), tables_at(1), (x_twist_ref[0], x_twist_ref[1]))
        put(send, 2 * j, re)
        put(send, 2 * j + 1, im)

    def inverse_x(recv, j):
        re, im = get(recv, 2 * j, OWN_PAD), get(recv, 2 * j + 1, OWN_PAD)
        return x_inverse(re, im, tables_at(2), tables_at(3), (x_twist_ref[0], x_twist_ref[1]))

    y_twist = lambda: (y_twist_ref[0], y_twist_ref[1])

    def forward_y(recv, j):
        re, im = get(recv, 2 * j, DEVS), get(recv, 2 * j + 1, DEVS)
        return y_forward(re, im, tables_at(4), tables_at(5), y_twist())

    def inverse_y(re, im, send, j):
        re, im = y_inverse(re, im, tables_at(6), tables_at(7), y_twist())
        put(send, 2 * j, re)
        put(send, 2 * j + 1, im)

    vel_copy.wait()
    lane = lax.broadcasted_iota(jnp.int32, (64, LANES), 1)
    pack_y[0] = vel[:, 63, :]
    pack_y[1] = vel[:, 0, :]

    def pack(b, carry):
        last, first = carry
        value = vel[b]
        last = jnp.where(lane == b, pltpu.roll(value, b + 1, axis=1), last)
        first = jnp.where(lane == b, pltpu.roll(value, b, axis=1), first)
        return last, first

    zero = jnp.zeros((64, LANES), F32)
    last, first = lax.fori_loop(0, 3 * LZ, pack, (zero, zero))
    pack_x[0] = last
    pack_x[1] = first
    up_r, down_r = lax.rem(row + 1, ROWS), lax.rem(row + ROWS - 1, ROWS)
    up_c, down_c = lax.rem(col + 1, COLS), lax.rem(col + COLS - 1, COLS)
    halos = [
        remote(pack_y.at[0], low_y, halo_sems.at[0], halo_sems.at[4], (up_r, col)),
        remote(pack_y.at[1], high_y, halo_sems.at[1], halo_sems.at[5], (down_r, col)),
        remote(pack_x.at[0], low_x, halo_sems.at[2], halo_sems.at[6], (row, up_c)),
        remote(pack_x.at[1], high_x, halo_sems.at[3], halo_sems.at[7], (row, down_c)),
    ]
    for h in halos:
        h.start()

    for f in range(2):
        wait_bytes(lines.at[f], recv_sems.at[f])
        fields[f] = jnp.transpose(lines[f].reshape(LANES, 256))
        forward_x(f, send1, f)
    to_owners(send1, recv1, 2)

    @pl.when(is_owner)
    def _():
        wait_bytes(recv1, recv_sems.at[2])
        kx, ky, mag, weight = wave_grids(my_p)
        for f in range(2):
            re, im = forward_y(recv1, f)
            spec[2 * f] = re * weight
            spec[2 * f + 1] = im * weight
        inverse_y(spec[0] * mag, spec[1] * mag, send2, 0)
        to_lines(send2, recv2, 3)
        turned[0] = mag * mag * spec[0]
        turned[1] = mag * mag * spec[1]
        turned[2] = mag * mag * mag * spec[0]
        turned[3] = mag * mag * mag * spec[1]
        for f in range(2):
            turned[4 + 4 * f] = -kx * spec[2 * f + 1]
            turned[5 + 4 * f] = kx * spec[2 * f]
            turned[6 + 4 * f] = -ky * spec[2 * f + 1]
            turned[7 + 4 * f] = ky * spec[2 * f]
        for j in range(6):
            inverse_y(turned[2 * j], turned[2 * j + 1], send2b, j)
        to_lines(send2b, recv2b, 4)

    wait_bytes(recv2.at[:OWNERS], recv_sems.at[3])
    vert = inverse_x(recv2, 0)
    fields[2] = vert
    fields[0] = -fields[1] * vert
    forward_x(0, send3, 0)
    to_owners(send3, recv3, 5)

    @pl.when(is_owner)
    def _():
        wait_bytes(recv3, recv_sems.at[5])
        kx, ky, mag, weight = wave_grids(my_p)
        re, im = forward_y(recv3, 0)
        first_factor = weight * mag
        second_factor = first_factor * mag
        inverse_y(re * first_factor, im * first_factor, send4, 0)
        inverse_y(re * second_factor, im * second_factor, send4, 1)
        to_lines(send4, recv4, 6)

    wait_bytes(recv2b.at[:OWNERS], recv_sems.at[4])
    for j in range(6):
        fields[3 + j] = inverse_x(recv2b, j)

    wait_bytes(recv4.at[:OWNERS], recv_sems.at[6])
    vert_two = inverse_x(recv4, 0)
    eta = fields[1]
    fields[0] = -eta * vert_two - 0.5 * eta * eta * fields[3]
    forward_x(0, send5, 0)
    to_owners(send5, recv5, 7)

    @pl.when(is_owner)
    def _():
        wait_bytes(recv5, recv_sems.at[7])
        kx, ky, mag, weight = wave_grids(my_p)
        re, im = forward_y(recv5, 0)
        factor = weight * mag
        inverse_y(re * factor, im * factor, send6, 0)
        to_lines(send6, recv6, 8)

    curve_two = inverse_x(recv4, 1)
    eta = fields[1]
    fields[2] = fields[2] + vert_two + eta * (fields[3] + curve_two) + 0.5 * eta * eta * fields[4]
    pot_dx, pot_dy, height_dx, height_dy = (fields[5 + j] for j in range(4))
    fields[7] = 1.0 + (height_dx * height_dx + height_dy * height_dy)
    fields[3] = -(height_dx * pot_dx + height_dy * pot_dy)
    fields[4] = -GRAVITY * eta - 0.5 * (pot_dx * pot_dx + pot_dy * pot_dy)

    def coarsen(j):
        hi, lo = split(out_t[j])
        spec[0] = dot(hi, pairs_ref[...]) + dot(lo, pairs_ref[...])
        return spec[0, pl.ds(0, 64, stride=2), :] + spec[0, pl.ds(1, 64, stride=2), :]

    out_t[2] = jnp.transpose(pot_dx)
    out_t[3] = jnp.transpose(pot_dy)
    coarse_t[0] = coarsen(2)
    coarse_t[1] = coarsen(3)

    wait_bytes(recv6.at[:OWNERS], recv_sems.at[8])
    vertical = fields[2] + inverse_x(recv6, 0)
    scaled = fields[7] * vertical
    height_rate = fields[3] + scaled
    out_t[0] = jnp.transpose(height_rate)
    out_t[1] = jnp.transpose(fields[4] + 0.5 * scaled * vertical)
    out_t[2] = jnp.transpose(GRAVITY * (fields[1] + SURFACE_STEP * height_rate))
    pressure = coarsen(2)
    coarse_t[2] = pressure
    lane64 = lax.broadcasted_iota(jnp.int32, (64, LANES), 1)
    east = pltpu.roll(pressure, LANES - 1, axis=1)
    east = jnp.where(lane64 == LANES - 1, pltpu.roll(east, 56, axis=0), east)
    west = pltpu.roll(pressure, 1, axis=1)
    west = jnp.where(lane64 == 0, pltpu.roll(west, 8, axis=0), west)
    coarse_t[3] = 0.5 * (east - west)

    def pieces(to):
        fine = pl.ds(to * LINES, LINES)
        few = pl.ds(to * 8, 8)
        mine = pl.ds(col * LINES, LINES)
        my_few = pl.ds(col * 8, 8)
        return [
            (out_t.at[0, fine, :], height_out.at[mine, :]),
            (out_t.at[1, fine, :], pot_out.at[mine, :]),
            (coarse_t.at[0, few, :], su_out.at[my_few, :]),
            (coarse_t.at[1, few, :], sv_out.at[my_few, :]),
            (coarse_t.at[3, few, :], lx_out.at[my_few, :]),
            (coarse_t.at[2, few, :], press_out.at[pl.ds(col * 8 + 8, 8), :]),
        ]

    for i in range(1, COLS):
        to = lax.rem(col + i, COLS)
        for k, (src, dst) in enumerate(pieces(to)):
            remote(src, dst, out_sems.at[k], out_sems.at[6 + k], (row, to)).start()
    for k, (src, dst) in enumerate(pieces(col)):
        pltpu.make_async_copy(src, dst, out_sems.at[6 + k]).start()

    @pl.when(col == COLS - 1)
    def _():
        for to in range(COLS):
            remote(
                coarse_t.at[2, pl.ds(to * 8, 8), :],
                press_out.at[pl.ds(0, 8), :],
                out_sems.at[12],
                out_sems.at[11],
                (up_r, to),
            ).start()

    @pl.when(col == 0)
    def _():
        for to in range(COLS):
            remote(
                coarse_t.at[2, pl.ds(to * 8, 8), :],
                press_out.at[pl.ds(72, 8), :],
                out_sems.at[12],
                out_sems.at[11],
                (down_r, to),
            ).start()

    for k, ref in enumerate((height_out, pot_out, su_out, sv_out, lx_out, press_out)):
        wait_bytes(ref, out_sems.at[6 + k])

    for h in halos:
        h.wait()
    for f in range(2):
        wait_bytes(lines.at[f, :7], send_sems.at[f])
    for k in range(2):
        wait_bytes(out_t.at[k, :112, :], out_sems.at[k])
    for k in range(4):
        wait_bytes(coarse_t.at[k, :56, :], out_sems.at[2 + k])

    @pl.when((col == 0) | (col == COLS - 1))
    def _():
        wait_bytes(coarse_t.at[2], out_sems.at[12])

    @pl.when(is_owner)
    def _():
        for buf, k in ((send1, 2), (send3, 5), (send5, 7)):
            wait_bytes(buf.at[: OWNERS - 1], send_sems.at[k])
        for buf, k in ((send2, 3), (send2b, 4), (send4, 6), (send6, 8)):
            wait_bytes(buf.at[: DEVS - 1], send_sems.at[k])

    @pl.when(jnp.logical_not(is_owner))
    def _():
        for buf, k in ((send1, 2), (send3, 5), (send5, 7)):
            wait_bytes(buf.at[:OWNERS], send_sems.at[k])


def flow_kernel(vel, su_ref, sv_ref, lx_ref, press, low_y, high_y, low_x, high_x, out):
    shape = (64, LANES)
    lane = lax.broadcasted_iota(jnp.int32, shape, 1)
    line = lax.broadcasted_iota(jnp.int32, shape, 0)
    su, sv = su_ref[...], sv_ref[...]
    load_x = lx_ref[...]
    load_y = 0.5 * (press[9:73, :] - press[7:71, :])
    from_low, from_high = low_x[...], high_x[...]

    def derivs(q, l, top):
        b = q * LZ + l
        mid = vel[b]
        above = jnp.where(l == 0, top, vel[q * LZ + jnp.maximum(l - 1, 0)])
        below = vel[q * LZ + jnp.minimum(l + 1, LZ - 1)]
        east = jnp.where(
            lane == LANES - 1,
            pltpu.roll(from_high, LANES - 1 - b, axis=1),
            pltpu.roll(mid, LANES - 1, axis=1),
        )
        west = jnp.where(
            lane == 0,
            pltpu.roll(from_low, lax.rem(LANES - b, LANES), axis=1),
            pltpu.roll(mid, 1, axis=1),
        )
        north = jnp.where(line == 63, high_y[pl.ds(b, 1), :], pltpu.roll(mid, 63, axis=0))
        south = jnp.where(line == 0, low_y[pl.ds(b, 1), :], pltpu.roll(mid, 1, axis=0))
        lap = east + west + north + south + above + below - 6.0 * mid
        return mid, 0.5 * (east - west), 0.5 * (north - south), 0.5 * (above - below), lap

    def level(l, _):
        depth = jnp.full(shape, l, jnp.int32).astype(F32) + 0.5
        load_decay = jnp.exp(-DECAY_RATE * depth)
        drift_decay = jnp.exp(-2.0 * DECAY_RATE * depth)
        u, u_dx, u_dy, u_dz, u_lap = derivs(0, l, su)
        v, v_dx, v_dy, v_dz, v_lap = derivs(1, l, sv)
        w, w_dx, w_dy, w_dz, w_lap = derivs(2, l, jnp.zeros(shape, F32))
        vort_x = w_dy - v_dz
        vort_y = u_dz - w_dx
        vort_z = v_dx - u_dy
        drift_u = su * drift_decay
        drift_v = sv * drift_decay

        def advance(mid, dx, dy, dz, lap, force):
            carried = u * dx + v * dy + w * dz
            return mid + FLOW_STEP * (-carried + VISCOSITY * lap + force)

        out[l] = advance(u, u_dx, u_dy, u_dz, u_lap, drift_v * vort_z - load_x * load_decay)
        out[LZ + l] = advance(v, v_dx, v_dy, v_dz, v_lap, -drift_u * vort_z - load_y * load_decay)
        out[2 * LZ + l] = advance(w, w_dx, w_dy, w_dz, w_lap, drift_u * vort_y - drift_v * vort_x)
        return 0

    lax.fori_loop(0, LZ, level, 0)


def local(surface_height, surface_potential, velocity):
    flow = velocity.reshape(3 * LZ, 64, LANES)
    tabs = [jnp.asarray(t) for t in tables()]
    in_vmem = pl.BlockSpec(memory_space=VMEM)

    def shape(*dims):
        return jax.ShapeDtypeStruct(dims, F32)

    def buf(*dims):
        return VMEM(dims, F32)

    messages = []
    for kind, count in (("o", 4), ("l", 2), ("l", 12), ("o", 2), ("l", 4), ("o", 2), ("l", 2)):
        if kind == "o":
            messages += [buf(OWN_PAD, count, LANES), buf(DEVS, count, LANES)]
        else:
            messages += [buf(DEVS, count, LANES), buf(OWN_PAD, count, LANES)]
    outs = pl.pallas_call(
        surface_kernel,
        name="surface",
        out_shape=[
            shape(128, 256),
            shape(128, 256),
            shape(64, LANES),
            shape(64, LANES),
            shape(64, LANES),
            shape(80, LANES),
            shape(48, LANES),
            shape(48, LANES),
            shape(64, LANES),
            shape(64, LANES),
        ],
        in_specs=[in_vmem, in_vmem, pl.BlockSpec(memory_space=pl.ANY)] + [in_vmem] * len(tabs),
        out_specs=[in_vmem] * 10,
        scratch_shapes=[buf(2, COLS, LINES, 256), buf(9, 256, LANES)]
        + messages
        + [
            buf(4, LANES, LANES),
            buf(12, LANES, LANES),
            buf(4, LANES, 256),
            buf(4, 64, LANES),
            buf(48, 64, LANES),
            buf(2, 48, LANES),
            buf(2, 64, LANES),
            pltpu.SemaphoreType.DMA,
            pltpu.SemaphoreType.DMA((9,)),
            pltpu.SemaphoreType.DMA((9,)),
            pltpu.SemaphoreType.DMA((13,)),
            pltpu.SemaphoreType.DMA((8,)),
        ],
        compiler_params=pltpu.CompilerParams(
            collective_id=0, has_side_effects=True, vmem_limit_bytes=56 * 1024 * 1024
        ),
    )(surface_potential, surface_height, flow, *tabs)
    height_rate, potential_rate = outs[:2]
    nxt = pl.pallas_call(
        flow_kernel,
        name="flow",
        out_shape=shape(3 * LZ, 64, LANES),
        in_specs=[in_vmem] * 9,
        out_specs=in_vmem,
        compiler_params=pltpu.CompilerParams(vmem_limit_bytes=32 * 1024 * 1024),
    )(flow, *outs[2:])
    return height_rate, potential_rate, nxt.reshape(velocity.shape)


def solution(mesh):
    specs = (P("row", "col"), P("row", "col"), P(None, None, "row", "col"))
    return jax.shard_map(local, mesh=mesh, in_specs=specs, out_specs=specs, check_vma=False)
```

```python
import functools

import jax
import jax.numpy as jnp
import numpy as np
from jax import lax
from jax.experimental import pallas as pl
from jax.experimental.pallas import tpu as pltpu
from jax.sharding import PartitionSpec as P

N = 2048
KEPT = N // 3
ROWS = 16
COLS = 8
DEVS = ROWS * COLS
LINES = 16
OWNERS = 86
OWN_PAD = 88
LANES = 128
LZ = 16
GRAVITY = 1.0
SURFACE_STEP = 0.05
FLOW_STEP = 0.5
VISCOSITY = 0.2
DECAY_RATE = 0.05
LOGICAL = pl.DeviceIdType.LOGICAL
EARLY_LEVELS = 8
F32 = jnp.float32
BF16 = jnp.bfloat16
VMEM = pltpu.VMEM


def block_complex(c, s):
    return np.block([[c, -s], [s, c]])


def split_table(t):
    hi = t.astype(np.float32).astype(jnp.bfloat16)
    lo = (t - hi.astype(np.float64)).astype(np.float32).astype(jnp.bfloat16)
    return hi, lo


@functools.cache
def tables():
    def wave(a, b, n):
        ang = 2.0 * np.pi * ((a[:, None] * b[None, :]) % n) / n
        return np.cos(ang), np.sin(ang)

    r8, r16, r128, r256 = (np.arange(k) for k in (8, 16, 128, 256))
    own = np.arange(OWN_PAD)
    eye16, eye8 = np.eye(16), np.eye(8)
    c8, s8 = wave(r8, r8, 8)
    c16, s16 = wave(r16, r16, 16)
    x_first = np.concatenate([np.kron(c8, eye16), np.kron(-s8, eye16)], axis=1)
    x_last = np.concatenate([np.kron(c8, eye16), np.kron(-s8, eye16)], axis=0)
    cp, sp = wave(own, r256, 256)
    x_second = block_complex(cp, -sp)
    x_third = block_complex(cp.T, sp.T)
    c1, s1 = wave(r128, r128, 128)
    y_first = block_complex(c1, -s1)
    y_last = block_complex(c1, s1)
    y_second = block_complex(np.kron(eye8, c16), np.kron(eye8, s16))
    y_third = block_complex(np.kron(eye8, c16), np.kron(eye8, -s16))
    ct, st = wave(r256, r8, N)
    x_twist = np.stack([np.repeat(ct, 16, axis=1), np.repeat(st, 16, axis=1)])
    ct, st = wave(r128, r16, N)
    y_twist = np.stack([np.tile(ct, (1, 8)), np.tile(st, (1, 8))])
    pairs = np.kron(np.eye(128), np.ones((2, 1))) * 0.25
    mats = [x_first, x_second, x_third, x_last, y_first, y_second, y_third, y_last]
    out = []
    for m in mats:
        out.extend(split_table(m))
    out.append(pairs.astype(np.float32).astype(jnp.bfloat16))
    out.append(x_twist.astype(np.float32))
    out.append(y_twist.astype(np.float32))
    return tuple(out)


def split(a):
    hi = a.astype(BF16)
    return hi, (a - hi.astype(F32)).astype(BF16)


def dot(a, b):
    return lax.dot_general(a, b, (((1,), (0,)), ((), ())), preferred_element_type=F32)


def left_table(table, data):
    th, tl = table
    dh, dl = split(data)
    return dot(th, dh) + dot(th, dl) + dot(tl, dh)


def right_table(data, table):
    th, tl = table
    dh, dl = split(data)
    return dot(dh, th) + dot(dl, th) + dot(dh, tl)


def x_forward(phys, first, second, twist):
    z = right_table(phys, first)
    zr, zi = z[:, :LANES], z[:, LANES:]
    c, s = twist
    t = jnp.concatenate([zr * c + zi * s, zi * c - zr * s], axis=0)
    out = left_table(second, t)
    return out[:OWN_PAD], out[OWN_PAD:]


def x_inverse(re, im, third, last, twist):
    u = left_table(third, jnp.concatenate([re, im], axis=0))
    ur, ui = u[:256], u[256:]
    c, s = twist
    t = jnp.concatenate([ur * c - ui * s, ur * s + ui * c], axis=1)
    return right_table(t, last)


def y_forward(re, im, first, second, twist):
    t = left_table(first, jnp.concatenate([re, im], axis=0))
    tr, ti = t[:LANES], t[LANES:]
    c, s = twist
    z = right_table(jnp.concatenate([tr * c + ti * s, ti * c - tr * s], axis=1), second)
    return z[:, :LANES], z[:, LANES:]


def y_inverse(re, im, third, last, twist):
    u = right_table(jnp.concatenate([re, im], axis=1), third)
    ur, ui = u[:, :LANES], u[:, LANES:]
    c, s = twist
    out = left_table(last, jnp.concatenate([ur * c - ui * s, ur * s + ui * c], axis=0))
    return out[:LANES], out[LANES:]


def wave_grids(p):
    lane = lax.broadcasted_iota(jnp.int32, (LANES, LANES), 1)
    q1 = lax.broadcasted_iota(jnp.int32, (LANES, LANES), 0)
    kx_index = lane // 16 + 8 * p
    ky_index = q1 + 128 * (lane % 16)
    ky_signed = jnp.where(ky_index < N // 2, ky_index, ky_index - N)
    unit = np.float32(2.0 * np.pi / N)
    kx = unit * kx_index.astype(F32)
    ky = unit * ky_signed.astype(F32)
    kept = (jnp.abs(ky_signed) <= KEPT) & (kx_index <= KEPT)
    fold = jnp.where(kx_index == 0, 1.0, 2.0) / float(N * N)
    weight = jnp.where(kept, fold, 0.0).astype(F32)
    return kx, ky, jnp.sqrt(kx * kx + ky * ky), weight


def get(buf, j, count):
    return buf[:count, j, :]


def put(buf, j, value):
    buf[: value.shape[0], j, :] = value


def far_first():
    hops = (0, 1, 2, 1)
    offsets = [(a, b, c) for a in range(4) for b in range(4) for c in range(4)]
    return sorted(offsets, key=lambda o: -(hops[o[0]] + hops[o[1]] + hops[o[2]]))


def surface_kernel(*refs):
    phi_ref, eta_ref, vel_ref = refs[:3]
    n_tab = 19
    tab_in = refs[3 : 3 + n_tab]
    at = 3 + n_tab
    height_out, pot_out, lx_out, press_out, base_out = refs[at : at + 5]
    at += 5
    tab = refs[at : at + n_tab]
    at += n_tab
    (
        lines,
        fields,
        send1,
        recv1,
        send1b,
        recv1b,
        send2,
        recv2,
        send2b,
        recv2b,
        send2c,
        recv2c,
        send3,
        recv3,
        send4,
        recv4,
        send4b,
        recv4b,
        send5,
        recv5,
        send6,
        recv6,
        spec,
        out_t,
        coarse_t,
        vel,
        base,
        pack_y,
        pack_x,
        low_y,
        high_y,
        low_x,
        high_x,
        su_tile,
        sv_tile,
        ids,
        own_ids,
        own_ps,
        load_sems,
        send_sems,
        recv_sems,
        out_sems,
        halo_sems,
    ) = refs[at:]
    row, col = lax.axis_index("row"), lax.axis_index("col")
    me = row * COLS + col
    is_owner = me % 3 != 2
    my_p = me - me // 3

    def remote(src, dst, send_sem, recv_sem, place):
        return pltpu.make_async_remote_copy(
            src_ref=src,
            dst_ref=dst,
            send_sem=send_sem,
            recv_sem=recv_sem,
            device_id=place,
            device_id_type=LOGICAL,
        )

    def wait_bytes(ref, sem):
        pltpu.make_async_copy(ref, ref, sem).wait()

    barrier = pltpu.get_barrier_semaphore()
    for i in range(1, COLS):
        pl.semaphore_signal(
            barrier, inc=1, device_id=row * COLS + (col + i) % COLS, device_id_type=LOGICAL
        )
    for i in range(1, ROWS):
        pl.semaphore_signal(
            barrier, inc=1, device_id=((row + i) % ROWS) * COLS + col, device_id_type=LOGICAL
        )
    vel_copy = pltpu.make_async_copy(vel_ref, vel, load_sems.at[n_tab])
    vel_copy.start()
    loads = [
        pltpu.make_async_copy(src, dst, load_sems.at[k])
        for k, (src, dst) in enumerate(zip(tab_in, tab))
    ]
    for load in loads:
        load.start()

    x_at = (col % 2) * 2 + row // 8
    y_at = (row // 2) % 4
    z_at = col // 2
    x_part = [((x_at + d) % 4) % 2 * 64 + ((x_at + d) % 4) // 2 for d in range(4)]
    y_part = [((y_at + d) % 4) * 16 for d in range(4)]
    z_part = [((z_at + d) % 4) * 2 for d in range(4)]
    core = row % 2
    cores = (8 * (1 - core), 8 * core)
    slot = jnp.int32(0)
    entry = 0
    for dx, dy, dz in far_first():
        chip = x_part[dx] + y_part[dy] + z_part[dz]
        for side in cores:
            place = chip + side
            third = place // 3
            ids[entry] = place
            own_ids[slot] = place
            own_ps[slot] = place - third
            slot = slot + (place - 3 * third < 2).astype(jnp.int32)
            entry += 1

    for buf in (recv2, recv2b, recv2c, recv4, recv4b, recv6):
        buf[OWNERS:OWN_PAD] = jnp.zeros((OWN_PAD - OWNERS,) + buf.shape[1:], F32)
    pl.semaphore_wait(barrier, COLS + ROWS - 2)

    for f, ref in enumerate((phi_ref, eta_ref)):
        for i in (4, 5, 3, 6, 2, 7, 1):
            to = (col + i) % COLS
            remote(
                ref.at[pl.ds(to * LINES, LINES), :],
                lines.at[f, col],
                send_sems.at[f],
                recv_sems.at[f],
                row * COLS + to,
            ).start()
        pltpu.make_async_copy(
            ref.at[pl.ds(col * LINES, LINES), :], lines.at[f, col], recv_sems.at[f]
        ).start()

    def to_owners(send, recv, k):
        def step(i, _):
            remote(
                send.at[own_ps[i]], recv.at[me], send_sems.at[k], recv_sems.at[k], own_ids[i]
            ).start()
            return 0

        lax.fori_loop(0, OWNERS - 1, step, 0, unroll=5)

        @pl.when(is_owner)
        def _():
            pltpu.make_async_copy(send.at[my_p], recv.at[me], recv_sems.at[k]).start()

        @pl.when(jnp.logical_not(is_owner))
        def _():
            step(OWNERS - 1, 0)

    def to_lines(send, recv, k):
        def step(i, _):
            other = ids[i]
            remote(
                send.at[other], recv.at[my_p], send_sems.at[k], recv_sems.at[k], other
            ).start()
            return 0

        lax.fori_loop(0, DEVS - 2, step, 0, unroll=6)
        step(DEVS - 2, 0)
        pltpu.make_async_copy(send.at[me], recv.at[my_p], recv_sems.at[k]).start()

    def tables_at(k):
        return tab[2 * k][...], tab[2 * k + 1][...]

    pairs_ref, x_twist_ref, y_twist_ref = tab[16:19]

    def forward_x(phys, send):
        re, im = x_forward(phys, tables_at(0), tables_at(1), (x_twist_ref[0], x_twist_ref[1]))
        put(send, 0, re)
        put(send, 1, im)

    def inverse_x(recv, j):
        re, im = get(recv, 2 * j, OWN_PAD), get(recv, 2 * j + 1, OWN_PAD)
        return x_inverse(re, im, tables_at(2), tables_at(3), (x_twist_ref[0], x_twist_ref[1]))

    def forward_y(recv):
        re, im = get(recv, 0, DEVS), get(recv, 1, DEVS)
        return y_forward(re, im, tables_at(4), tables_at(5), (y_twist_ref[0], y_twist_ref[1]))

    def inverse_y(re, im, send, j):
        re, im = y_inverse(re, im, tables_at(6), tables_at(7), (y_twist_ref[0], y_twist_ref[1]))
        put(send, 2 * j, re)
        put(send, 2 * j + 1, im)

    for load in loads:
        load.wait()

    wait_bytes(lines.at[0], recv_sems.at[0])
    forward_x(jnp.transpose(lines[0].reshape(LANES, 256)), send1)
    to_owners(send1, recv1, 2)
    wait_bytes(lines.at[1], recv_sems.at[1])
    fields[1] = jnp.transpose(lines[1].reshape(LANES, 256))
    forward_x(fields[1], send1b)
    to_owners(send1b, recv1b, 3)

    vel_copy.wait()
    lane = lax.broadcasted_iota(jnp.int32, (64, LANES), 1)
    line = lax.broadcasted_iota(jnp.int32, (64, LANES), 0)
    pack_y[0] = vel[:, 63, :]
    pack_y[1] = vel[:, 0, :]

    def pack(b, carry):
        last, first = carry
        value = vel[b]
        last = jnp.where(lane == b, pltpu.roll(value, b + 1, axis=1), last)
        first = jnp.where(lane == b, pltpu.roll(value, b, axis=1), first)
        return last, first

    zero = jnp.zeros((64, LANES), F32)
    last, first = lax.fori_loop(0, 3 * LZ, pack, (zero, zero))
    pack_x[0] = last
    pack_x[1] = first
    up_r, down_r = (row + 1) % ROWS, (row + ROWS - 1) % ROWS
    up_c, down_c = (col + 1) % COLS, (col + COLS - 1) % COLS
    halos = [
        remote(pack_y.at[0], low_y, halo_sems.at[0], halo_sems.at[4], up_r * COLS + col),
        remote(pack_y.at[1], high_y, halo_sems.at[1], halo_sems.at[5], down_r * COLS + col),
        remote(pack_x.at[0], low_x, halo_sems.at[2], halo_sems.at[6], row * COLS + up_c),
        remote(pack_x.at[1], high_x, halo_sems.at[3], halo_sems.at[7], row * COLS + down_c),
    ]
    for h in halos:
        h.start()

    @pl.when(is_owner)
    def _():
        kx, ky, mag, weight = wave_grids(my_p)
        wait_bytes(recv1, recv_sems.at[2])
        re, im = forward_y(recv1)
        spec[0] = re * weight
        spec[1] = im * weight
        inverse_y(spec[0] * mag, spec[1] * mag, send2, 0)
        to_lines(send2, recv2, 4)
        square = mag * mag
        inverse_y(spec[0] * square, spec[1] * square, send2b, 0)
        inverse_y(-kx * spec[1], kx * spec[0], send2b, 1)
        inverse_y(-ky * spec[1], ky * spec[0], send2b, 2)
        to_lines(send2b, recv2b, 5)
        wait_bytes(recv1b, recv_sems.at[3])
        re, im = forward_y(recv1b)
        spec[2] = re * weight
        spec[3] = im * weight
        cube = square * mag
        inverse_y(spec[0] * cube, spec[1] * cube, send2c, 0)
        inverse_y(-kx * spec[3], kx * spec[2], send2c, 1)
        inverse_y(-ky * spec[3], ky * spec[2], send2c, 2)
        to_lines(send2c, recv2c, 6)

    wait_bytes(recv2.at[:OWNERS], recv_sems.at[4])
    vert = inverse_x(recv2, 0)
    fields[2] = vert
    forward_x(-fields[1] * vert, send3)
    to_owners(send3, recv3, 7)

    def coarsen(j):
        hi, lo = split(out_t[j])
        spec[4] = dot(hi, pairs_ref[...]) + dot(lo, pairs_ref[...])
        return spec[4, pl.ds(0, 64, stride=2), :] + spec[4, pl.ds(1, 64, stride=2), :]

    wait_bytes(recv2b.at[:OWNERS], recv_sems.at[5])
    fields[3] = inverse_x(recv2b, 0)
    for j in range(2):
        slope = inverse_x(recv2b, 1 + j)
        fields[5 + j] = slope
        out_t[j] = jnp.transpose(slope)
        coarse_t[j] = coarsen(j)

    def spread(k, src, dst):
        for i in (4, 5, 3, 6, 2, 7, 1):
            to = (col + i) % COLS
            remote(src(to), dst, out_sems.at[k], out_sems.at[6 + k], row * COLS + to).start()
        pltpu.make_async_copy(src(col), dst, out_sems.at[6 + k]).start()

    few = lambda k: lambda to: coarse_t.at[k, pl.ds(to * 8, 8), :]
    fine = lambda k: lambda to: out_t.at[k, pl.ds(to * LINES, LINES), :]
    my_few, my_fine = pl.ds(col * 8, 8), pl.ds(col * LINES, LINES)
    spread(2, few(0), su_tile.at[my_few, :])
    spread(3, few(1), sv_tile.at[my_few, :])

    @pl.when(is_owner)
    def _():
        kx, ky, mag, weight = wave_grids(my_p)
        wait_bytes(recv3, recv_sems.at[7])
        re, im = forward_y(recv3)
        factor = weight * mag
        spec[0] = re * factor
        spec[1] = im * factor
        inverse_y(spec[0], spec[1], send4, 0)
        to_lines(send4, recv4, 8)
        inverse_y(spec[0] * mag, spec[1] * mag, send4b, 0)
        to_lines(send4b, recv4b, 9)

    wait_bytes(recv2c.at[:OWNERS], recv_sems.at[6])
    fields[4] = inverse_x(recv2c, 0)
    fields[7] = inverse_x(recv2c, 1)
    fields[8] = inverse_x(recv2c, 2)

    wait_bytes(recv4.at[:OWNERS], recv_sems.at[8])
    vert_two = inverse_x(recv4, 0)
    eta = fields[1]
    fields[2] = fields[2] + vert_two
    forward_x(-eta * vert_two - 0.5 * eta * eta * fields[3], send5)
    to_owners(send5, recv5, 10)

    for h in halos:
        h.wait()
    wait_bytes(su_tile, out_sems.at[8])
    wait_bytes(sv_tile, out_sems.at[9])

    def derivs(q, l, top):
        b = q * LZ + l
        mid = vel[b]
        above = jnp.where(l == 0, top, vel[q * LZ + jnp.maximum(l - 1, 0)])
        below = vel[q * LZ + jnp.minimum(l + 1, LZ - 1)]
        east = jnp.where(
            lane == LANES - 1,
            pltpu.roll(high_x[...], LANES - 1 - b, axis=1),
            pltpu.roll(mid, LANES - 1, axis=1),
        )
        west = jnp.where(
            lane == 0,
            pltpu.roll(low_x[...], (LANES - b) % LANES, axis=1),
            pltpu.roll(mid, 1, axis=1),
        )
        north = jnp.where(line == 63, high_y[pl.ds(b, 1), :], pltpu.roll(mid, 63, axis=0))
        south = jnp.where(line == 0, low_y[pl.ds(b, 1), :], pltpu.roll(mid, 1, axis=0))
        lap = east + west + north + south + above + below - 6.0 * mid
        return mid, 0.5 * (east - west), 0.5 * (north - south), 0.5 * (above - below), lap

    def level(l, _):
        depth = jnp.full((64, LANES), l, jnp.int32).astype(F32) + 0.5
        drift_decay = jnp.exp(-2.0 * DECAY_RATE * depth)
        u, u_dx, u_dy, u_dz, u_lap = derivs(0, l, su_tile[...])
        v, v_dx, v_dy, v_dz, v_lap = derivs(1, l, sv_tile[...])
        w, w_dx, w_dy, w_dz, w_lap = derivs(2, l, jnp.zeros((64, LANES), F32))
        vort_x = w_dy - v_dz
        vort_y = u_dz - w_dx
        vort_z = v_dx - u_dy
        drift_u = su_tile[...] * drift_decay
        drift_v = sv_tile[...] * drift_decay

        def advance(mid, dx, dy, dz, lap, force):
            carried = u * dx + v * dy + w * dz
            return mid + FLOW_STEP * (-carried + VISCOSITY * lap + force)

        base[l] = advance(u, u_dx, u_dy, u_dz, u_lap, drift_v * vort_z)
        base[LZ + l] = advance(v, v_dx, v_dy, v_dz, v_lap, -drift_u * vort_z)
        base[2 * LZ + l] = advance(w, w_dx, w_dy, w_dz, w_lap, drift_u * vort_y - drift_v * vort_x)
        return 0

    lax.fori_loop(0, EARLY_LEVELS, level, 0)

    @pl.when(is_owner)
    def _():
        kx, ky, mag, weight = wave_grids(my_p)
        wait_bytes(recv5, recv_sems.at[10])
        re, im = forward_y(recv5)
        factor = weight * mag
        inverse_y(re * factor, im * factor, send6, 0)
        to_lines(send6, recv6, 11)

    lax.fori_loop(EARLY_LEVELS, LZ, level, 0)
    base_copy = pltpu.make_async_copy(base, base_out, load_sems.at[n_tab + 1])
    base_copy.start()
    wait_bytes(recv4b.at[:OWNERS], recv_sems.at[9])
    curve_two = inverse_x(recv4b, 0)
    eta = fields[1]
    fields[2] = fields[2] + eta * (fields[3] + curve_two) + 0.5 * eta * eta * fields[4]
    pot_dx, pot_dy, height_dx, height_dy = (fields[5 + j] for j in range(4))
    fields[7] = 1.0 + (height_dx * height_dx + height_dy * height_dy)
    fields[3] = -(height_dx * pot_dx + height_dy * pot_dy)
    fields[4] = -GRAVITY * eta - 0.5 * (pot_dx * pot_dx + pot_dy * pot_dy)

    wait_bytes(recv6.at[:OWNERS], recv_sems.at[11])
    vertical = fields[2] + inverse_x(recv6, 0)
    scaled = fields[7] * vertical
    height_rate = fields[3] + scaled
    out_t[2] = jnp.transpose(height_rate)
    spread(0, fine(2), height_out.at[my_fine, :])
    out_t[3] = jnp.transpose(fields[4] + 0.5 * scaled * vertical)
    spread(1, fine(3), pot_out.at[my_fine, :])
    out_t[4] = jnp.transpose(GRAVITY * (fields[1] + SURFACE_STEP * height_rate))
    pressure = coarsen(4)
    coarse_t[2] = pressure
    spread(5, few(2), press_out.at[pl.ds(col * 8 + 8, 8), :])

    @pl.when(col == COLS - 1)
    def _():
        for to in range(COLS):
            remote(
                coarse_t.at[2, pl.ds(to * 8, 8), :],
                press_out.at[pl.ds(0, 8), :],
                out_sems.at[12],
                out_sems.at[11],
                up_r * COLS + to,
            ).start()

    @pl.when(col == 0)
    def _():
        for to in range(COLS):
            remote(
                coarse_t.at[2, pl.ds(to * 8, 8), :],
                press_out.at[pl.ds(72, 8), :],
                out_sems.at[12],
                out_sems.at[11],
                down_r * COLS + to,
            ).start()

    east = pltpu.roll(pressure, LANES - 1, axis=1)
    east = jnp.where(lane == LANES - 1, pltpu.roll(east, 56, axis=0), east)
    west = pltpu.roll(pressure, 1, axis=1)
    west = jnp.where(lane == 0, pltpu.roll(west, 8, axis=0), west)
    coarse_t[3] = 0.5 * (east - west)
    spread(4, few(3), lx_out.at[my_few, :])

    for f in range(2):
        wait_bytes(lines.at[f, :7], send_sems.at[f])
    for k in range(2):
        wait_bytes(out_t.at[k, :112, :], out_sems.at[k])
    for k in range(4):
        wait_bytes(coarse_t.at[k, :56, :], out_sems.at[2 + k])

    @pl.when((col == 0) | (col == COLS - 1))
    def _():
        wait_bytes(coarse_t.at[2], out_sems.at[12])

    owned = ((send1, 2), (send1b, 3), (send3, 7), (send5, 10))

    @pl.when(is_owner)
    def _():
        for buf, k in owned:
            wait_bytes(buf.at[: OWNERS - 1], send_sems.at[k])
        for buf, k in (
            (send2, 4),
            (send2b, 5),
            (send2c, 6),
            (send4, 8),
            (send4b, 9),
            (send6, 11),
        ):
            wait_bytes(buf.at[: DEVS - 1], send_sems.at[k])

    @pl.when(jnp.logical_not(is_owner))
    def _():
        for buf, k in owned:
            wait_bytes(buf.at[:OWNERS], send_sems.at[k])

    base_copy.wait()
    for k, ref in ((0, height_out), (1, pot_out), (4, lx_out), (5, press_out)):
        wait_bytes(ref, out_sems.at[6 + k])


CHUNK = 8


def load_kernel(base_in, lx_in, press_in, height_in, pot_in, out, height_out, pot_out, *scratch):
    base, load_x_buf, press, height, pot, in_sems, done_sems = scratch
    small = [
        pltpu.make_async_copy(src, dst, in_sems.at[k])
        for k, (src, dst) in enumerate(
            ((lx_in, load_x_buf), (press_in, press), (height_in, height), (pot_in, pot))
        )
    ]
    for copy in small[:2]:
        copy.start()
    chunks = 3 * LZ // CHUNK
    parts = [pl.ds(CHUNK * k, CHUNK) for k in range(chunks)]
    ins = [pltpu.make_async_copy(base_in.at[p], base.at[p], in_sems.at[4 + k]) for k, p in enumerate(parts)]
    outs = [pltpu.make_async_copy(base.at[p], out.at[p], done_sems.at[2 + k]) for k, p in enumerate(parts)]
    for copy in ins:
        copy.start()
    for copy in small[2:]:
        copy.start()
    small[0].wait()
    small[1].wait()
    loads = (load_x_buf[...], 0.5 * (press[9:73, :] - press[7:71, :]))
    for k in range(chunks):
        ins[k].wait()
        for b in range(CHUNK * k, CHUNK * k + CHUNK):
            q, l = divmod(b, LZ)
            if q < 2:
                decay = float(np.exp(-DECAY_RATE * (l + 0.5)))
                base[b] = base[b] - (FLOW_STEP * decay) * loads[q]
        outs[k].start()
    small[2].wait()
    last = [
        pltpu.make_async_copy(height, height_out, done_sems.at[0]),
        pltpu.make_async_copy(pot, pot_out, done_sems.at[1]),
    ]
    last[0].start()
    small[3].wait()
    last[1].start()
    for copy in outs + last:
        copy.wait()


def local(surface_height, surface_potential, velocity):
    flow = velocity.reshape(3 * LZ, 64, LANES)
    tabs = [jnp.asarray(t) for t in tables()]
    anywhere = pl.BlockSpec(memory_space=pl.ANY)

    def shape(*dims):
        return jax.ShapeDtypeStruct(dims, F32)

    def buf(*dims):
        return VMEM(dims, F32)

    messages = []
    for kind, count in zip("oolllollol", (2, 2, 2, 6, 6, 2, 2, 2, 2, 2)):
        if kind == "o":
            messages += [buf(OWN_PAD, count, LANES), buf(DEVS, count, LANES)]
        else:
            messages += [buf(DEVS, count, LANES), buf(OWN_PAD, count, LANES)]
    outs = pl.pallas_call(
        surface_kernel,
        name="surface",
        out_shape=[
            shape(128, 256),
            shape(128, 256),
            shape(64, LANES),
            shape(80, LANES),
            shape(3 * LZ, 64, LANES),
        ],
        in_specs=[anywhere] * (3 + len(tabs)),
        out_specs=[anywhere] * 5,
        scratch_shapes=[VMEM(t.shape, t.dtype) for t in tabs]
        + [buf(2, COLS, LINES, 256), buf(9, 256, LANES)]
        + messages
        + [
            buf(5, LANES, LANES),
            buf(5, LANES, 256),
            buf(4, 64, LANES),
            buf(3 * LZ, 64, LANES),
            buf(3 * LZ, 64, LANES),
            buf(2, 48, LANES),
            buf(2, 64, LANES),
            buf(48, LANES),
            buf(48, LANES),
            buf(64, LANES),
            buf(64, LANES),
            buf(64, LANES),
            buf(64, LANES),
            pltpu.SMEM((DEVS,), jnp.int32),
            pltpu.SMEM((DEVS,), jnp.int32),
            pltpu.SMEM((DEVS,), jnp.int32),
            pltpu.SemaphoreType.DMA((len(tabs) + 2,)),
            pltpu.SemaphoreType.DMA((12,)),
            pltpu.SemaphoreType.DMA((12,)),
            pltpu.SemaphoreType.DMA((13,)),
            pltpu.SemaphoreType.DMA((8,)),
        ],
        compiler_params=pltpu.CompilerParams(
            collective_id=0, has_side_effects=True, vmem_limit_bytes=56 * 1024 * 1024
        ),
    )(surface_potential, surface_height, flow, *tabs)
    height_rate, potential_rate, lx, press, base = outs
    nxt, height_rate, potential_rate = pl.pallas_call(
        load_kernel,
        name="load",
        out_shape=[shape(3 * LZ, 64, LANES), shape(128, 256), shape(128, 256)],
        in_specs=[anywhere] * 5,
        out_specs=[anywhere] * 3,
        scratch_shapes=[
            buf(3 * LZ, 64, LANES),
            buf(64, LANES),
            buf(80, LANES),
            buf(128, 256),
            buf(128, 256),
            pltpu.SemaphoreType.DMA((4 + 3 * LZ // CHUNK,)),
            pltpu.SemaphoreType.DMA((2 + 3 * LZ // CHUNK,)),
        ],
    )(base, lx, press, height_rate, potential_rate)
    return height_rate, potential_rate, nxt.reshape(velocity.shape)


def solution(mesh):
    specs = (P("row", "col"), P("row", "col"), P(None, None, "row", "col"))
    return jax.shard_map(local, mesh=mesh, in_specs=specs, out_specs=specs, check_vma=False)
```

```python
import functools

import jax
import jax.numpy as jnp
import numpy as np
from jax import lax
from jax.experimental import pallas as pl
from jax.experimental.pallas import tpu as pltpu
from jax.sharding import PartitionSpec as P

N = 2048
KEPT = N // 3
ROWS = 16
COLS = 8
DEVS = ROWS * COLS
LINES = 16
OWNERS = 86
OWN_PAD = 88
LANES = 128
LZ = 16
GRAVITY = 1.0
SURFACE_STEP = 0.05
FLOW_STEP = 0.5
VISCOSITY = 0.2
DECAY_RATE = 0.05
LOGICAL = pl.DeviceIdType.LOGICAL
EARLY_LEVELS = 12
SURFACE_VMEM = 20 * 1024 * 1024
LOAD_VMEM = 8 * 1024 * 1024
F32 = jnp.float32
BF16 = jnp.bfloat16
VMEM = pltpu.VMEM


def block_complex(c, s):
    return np.block([[c, -s], [s, c]])


def split_table(t):
    hi = t.astype(np.float32).astype(jnp.bfloat16)
    lo = (t - hi.astype(np.float64)).astype(np.float32).astype(jnp.bfloat16)
    return hi, lo


@functools.cache
def tables():
    def wave(a, b, n):
        ang = 2.0 * np.pi * ((a[:, None] * b[None, :]) % n) / n
        return np.cos(ang), np.sin(ang)

    r8, r16, r128, r256 = (np.arange(k) for k in (8, 16, 128, 256))
    own = np.arange(OWN_PAD)
    eye16, eye8 = np.eye(16), np.eye(8)
    c8, s8 = wave(r8, r8, 8)
    c16, s16 = wave(r16, r16, 16)
    x_first = np.concatenate([np.kron(c8, eye16), np.kron(-s8, eye16)], axis=1)
    x_last = np.concatenate([np.kron(c8, eye16), np.kron(-s8, eye16)], axis=0)
    cp, sp = wave(own, r256, 256)
    x_second = block_complex(cp, -sp)
    x_third = block_complex(cp.T, sp.T)
    c1, s1 = wave(r128, r128, 128)
    y_first = block_complex(c1, -s1)
    y_second = block_complex(np.kron(eye8, c16), np.kron(eye8, s16))
    ct, st = wave(r256, r8, N)
    x_twist = np.stack([np.repeat(ct, 16, axis=1), np.repeat(st, 16, axis=1)])
    ct, st = wave(r128, r16, N)
    y_twist = np.stack([np.tile(ct, (1, 8)), np.tile(st, (1, 8))])
    pairs = np.kron(np.eye(128), np.ones((2, 1))) * 0.25
    mats = [x_first, x_second, x_third, x_last, y_first, y_second]
    out = []
    for m in mats:
        out.extend(split_table(m))
    out.append(pairs.astype(np.float32).astype(jnp.bfloat16))
    out.append(x_twist.astype(np.float32))
    out.append(y_twist.astype(np.float32))
    return tuple(out)


def split(a):
    hi = a.astype(BF16)
    return hi, (a - hi.astype(F32)).astype(BF16)


def dot(a, b):
    return lax.dot_general(a, b, (((1,), (0,)), ((), ())), preferred_element_type=F32)


def left_table(table, data):
    th, tl = table
    dh, dl = split(data)
    both = dot(th, jnp.concatenate([dh, dl], axis=1))
    width = data.shape[1]
    return both[:, :width] + both[:, width:] + dot(tl, dh)


def right_table(data, table):
    th, tl = table
    dh, dl = split(data)
    return dot(dh, th) + dot(dl, th) + dot(dh, tl)


def x_forward(phys, first, second, twist):
    z = right_table(phys, first)
    zr, zi = z[:, :LANES], z[:, LANES:]
    c, s = twist
    t = jnp.concatenate([zr * c + zi * s, zi * c - zr * s], axis=0)
    out = left_table(second, t)
    return out[:OWN_PAD], out[OWN_PAD:]


def x_inverse(re, im, third, last, twist):
    u = left_table(third, jnp.concatenate([re, im], axis=0))
    ur, ui = u[:256], u[256:]
    c, s = twist
    t = jnp.concatenate([ur * c - ui * s, ur * s + ui * c], axis=1)
    return right_table(t, last)


def y_forward(re, im, first, second, twist):
    t = left_table(first, jnp.concatenate([re, im], axis=0))
    tr, ti = t[:LANES], t[LANES:]
    c, s = twist
    z = right_table(jnp.concatenate([tr * c + ti * s, ti * c - tr * s], axis=1), second)
    return z[:, :LANES], z[:, LANES:]


def y_inverse(re, im, first, second, twist):
    u = right_table(jnp.concatenate([re, -im], axis=1), second)
    ur, ui = u[:, :LANES], u[:, LANES:]
    c, s = twist
    out = left_table(first, jnp.concatenate([ur * c + ui * s, ui * c - ur * s], axis=0))
    return out[:LANES], -out[LANES:]


def wave_grids(p):
    lane = lax.broadcasted_iota(jnp.int32, (LANES, LANES), 1)
    q1 = lax.broadcasted_iota(jnp.int32, (LANES, LANES), 0)
    kx_index = lane // 16 + 8 * p
    ky_index = q1 + 128 * (lane % 16)
    ky_signed = jnp.where(ky_index < N // 2, ky_index, ky_index - N)
    unit = np.float32(2.0 * np.pi / N)
    kx = unit * kx_index.astype(F32)
    ky = unit * ky_signed.astype(F32)
    kept = (jnp.abs(ky_signed) <= KEPT) & (kx_index <= KEPT)
    fold = jnp.where(kx_index == 0, 1.0, 2.0) / float(N * N)
    weight = jnp.where(kept, fold, 0.0).astype(F32)
    return kx, ky, jnp.sqrt(kx * kx + ky * ky), weight


def get(buf, j, count):
    return buf[:count, j, :]


def put(buf, j, value):
    buf[: value.shape[0], j, :] = value


def far_first():
    hops = (0, 1, 2, 1)
    offsets = [(a, b, c) for a in range(4) for b in range(4) for c in range(4)]
    return sorted(offsets, key=lambda o: -(hops[o[0]] + hops[o[1]] + hops[o[2]]))


def surface_kernel(*refs):
    phi_ref, eta_ref, vel_ref = refs[:3]
    n_tab = 15
    tab_in = refs[3 : 3 + n_tab]
    at = 3 + n_tab
    (
        height_out,
        lx_out,
        press_out,
        base_out,
        stretch_out,
        advected_out,
        still_out,
    ) = refs[at : at + 7]
    at += 7
    tab = refs[at : at + n_tab]
    at += n_tab
    (
        lines,
        fields,
        send1,
        recv1,
        send1b,
        recv1b,
        send2,
        recv2,
        send2b,
        recv2b,
        send2c,
        recv2c,
        send2d,
        recv2d,
        send3,
        recv3,
        send4,
        recv4,
        send4b,
        recv4b,
        send5,
        recv5,
        send6,
        recv6,
        spec,
        out_t,
        coarse_t,
        vel,
        base,
        pack_y,
        pack_x,
        low_y,
        high_y,
        low_x,
        high_x,
        su_tile,
        sv_tile,
        ids,
        own_ids,
        own_ps,
        load_sems,
        send_sems,
        recv_sems,
        out_sems,
        early_sems,
        halo_sems,
    ) = refs[at:]
    row, col = lax.axis_index("row"), lax.axis_index("col")
    me = row * COLS + col
    is_owner = me % 3 != 2
    my_p = me - me // 3

    def remote(src, dst, send_sem, recv_sem, place):
        return pltpu.make_async_remote_copy(
            src_ref=src,
            dst_ref=dst,
            send_sem=send_sem,
            recv_sem=recv_sem,
            device_id=place,
            device_id_type=LOGICAL,
        )

    def wait_bytes(ref, sem):
        pltpu.make_async_copy(ref, ref, sem).wait()

    barrier = pltpu.get_barrier_semaphore()
    for i in range(1, COLS):
        pl.semaphore_signal(
            barrier, inc=1, device_id=row * COLS + (col + i) % COLS, device_id_type=LOGICAL
        )
    for i in range(1, ROWS):
        pl.semaphore_signal(
            barrier, inc=1, device_id=((row + i) % ROWS) * COLS + col, device_id_type=LOGICAL
        )
    vel_copy = pltpu.make_async_copy(vel_ref, vel, load_sems.at[n_tab])
    vel_copy.start()
    loads = [
        pltpu.make_async_copy(src, dst, load_sems.at[k])
        for k, (src, dst) in enumerate(zip(tab_in, tab))
    ]
    for load in loads:
        load.start()

    pl.semaphore_wait(barrier, COLS + ROWS - 2)

    for f, ref in enumerate((phi_ref, eta_ref)):
        for i in (5, 3, 7, 1, 4, 6, 2):
            to = (col + i) % COLS
            remote(
                ref.at[pl.ds(to * LINES, LINES), :],
                lines.at[f, col],
                send_sems.at[f],
                recv_sems.at[f],
                row * COLS + to,
            ).start()
        pltpu.make_async_copy(
            ref.at[pl.ds(col * LINES, LINES), :], lines.at[f, col], recv_sems.at[f]
        ).start()

    x_at = (col % 2) * 2 + row // 8
    y_at = (row // 2) % 4
    z_at = col // 2
    x_part = [((x_at + d) % 4) % 2 * 64 + ((x_at + d) % 4) // 2 for d in range(4)]
    y_part = [((y_at + d) % 4) * 16 for d in range(4)]
    z_part = [((z_at + d) % 4) * 2 for d in range(4)]
    core = row % 2
    cores = (8 * (1 - core), 8 * core)
    slot = jnp.int32(0)
    entry = 0
    for dx, dy, dz in far_first():
        chip = x_part[dx] + y_part[dy] + z_part[dz]
        for side in cores:
            place = chip + side
            third = place // 3
            ids[entry] = place
            own_ids[slot] = place
            own_ps[slot] = place - third
            slot = slot + (place - 3 * third < 2).astype(jnp.int32)
            entry += 1

    for buf in (recv2, recv2b, recv2c, recv2d, recv4, recv4b, recv6):
        buf[OWNERS:OWN_PAD] = jnp.zeros((OWN_PAD - OWNERS,) + buf.shape[1:], F32)
    def to_owners(send, recv, k):
        def step(i, _):
            remote(
                send.at[own_ps[i]], recv.at[me], send_sems.at[k], recv_sems.at[k], own_ids[i]
            ).start()
            return 0

        lax.fori_loop(0, OWNERS - 1, step, 0, unroll=5)

        @pl.when(is_owner)
        def _():
            pltpu.make_async_copy(send.at[my_p], recv.at[me], recv_sems.at[k]).start()

        @pl.when(jnp.logical_not(is_owner))
        def _():
            step(OWNERS - 1, 0)

    def to_lines(send, recv, k):
        def step(i, _):
            other = ids[i]
            remote(
                send.at[other], recv.at[my_p], send_sems.at[k], recv_sems.at[k], other
            ).start()
            return 0

        lax.fori_loop(0, DEVS - 2, step, 0, unroll=6)
        step(DEVS - 2, 0)
        pltpu.make_async_copy(send.at[me], recv.at[my_p], recv_sems.at[k]).start()

    def tables_at(k):
        return tab[2 * k][...], tab[2 * k + 1][...]

    pairs_ref, x_twist_ref, y_twist_ref = tab[12:15]

    def forward_x(phys, send):
        re, im = x_forward(phys, tables_at(0), tables_at(1), (x_twist_ref[0], x_twist_ref[1]))
        put(send, 0, re)
        put(send, 1, im)

    def inverse_x(recv, j):
        re, im = get(recv, 2 * j, OWN_PAD), get(recv, 2 * j + 1, OWN_PAD)
        return x_inverse(re, im, tables_at(2), tables_at(3), (x_twist_ref[0], x_twist_ref[1]))

    def forward_y(recv):
        re, im = get(recv, 0, DEVS), get(recv, 1, DEVS)
        return y_forward(re, im, tables_at(4), tables_at(5), (y_twist_ref[0], y_twist_ref[1]))

    def inverse_y(re, im, send, j):
        re, im = y_inverse(re, im, tables_at(4), tables_at(5), (y_twist_ref[0], y_twist_ref[1]))
        put(send, 2 * j, re)
        put(send, 2 * j + 1, im)

    for load in loads:
        load.wait()

    wait_bytes(lines.at[0], recv_sems.at[0])
    forward_x(jnp.transpose(lines[0].reshape(LANES, 256)), send1)
    to_owners(send1, recv1, 2)
    wait_bytes(lines.at[1], recv_sems.at[1])
    fields[1] = jnp.transpose(lines[1].reshape(LANES, 256))
    forward_x(fields[1], send1b)
    to_owners(send1b, recv1b, 3)

    vel_copy.wait()
    lane = lax.broadcasted_iota(jnp.int32, (64, LANES), 1)
    line = lax.broadcasted_iota(jnp.int32, (64, LANES), 0)
    pack_y[0] = vel[:, 63, :]
    pack_y[1] = vel[:, 0, :]

    def pack(b, carry):
        last, first = carry
        value = vel[b]
        last = jnp.where(lane == b, pltpu.roll(value, b + 1, axis=1), last)
        first = jnp.where(lane == b, pltpu.roll(value, b, axis=1), first)
        return last, first

    zero = jnp.zeros((64, LANES), F32)
    last, first = lax.fori_loop(0, 3 * LZ, pack, (zero, zero), unroll=8)
    pack_x[0] = last
    pack_x[1] = first
    up_r, down_r = (row + 1) % ROWS, (row + ROWS - 1) % ROWS
    up_c, down_c = (col + 1) % COLS, (col + COLS - 1) % COLS
    halos = [
        remote(pack_y.at[0], low_y, halo_sems.at[0], halo_sems.at[4], up_r * COLS + col),
        remote(pack_y.at[1], high_y, halo_sems.at[1], halo_sems.at[5], down_r * COLS + col),
        remote(pack_x.at[0], low_x, halo_sems.at[2], halo_sems.at[6], row * COLS + up_c),
        remote(pack_x.at[1], high_x, halo_sems.at[3], halo_sems.at[7], row * COLS + down_c),
    ]
    for h in halos:
        h.start()

    @pl.when(is_owner)
    def _():
        kx, ky, mag, weight = wave_grids(my_p)
        wait_bytes(recv1, recv_sems.at[2])
        re, im = forward_y(recv1)
        spec[0] = re * weight
        spec[1] = im * weight
        inverse_y(spec[0] * mag, spec[1] * mag, send2, 0)
        to_lines(send2, recv2, 4)
        square = mag * mag
        inverse_y(spec[0] * square, spec[1] * square, send2b, 0)
        to_lines(send2b, recv2b, 5)
        inverse_y(-kx * spec[1], kx * spec[0], send2c, 0)
        inverse_y(-ky * spec[1], ky * spec[0], send2c, 1)
        wait_bytes(recv1b, recv_sems.at[3])
        re, im = forward_y(recv1b)
        spec[2] = re * weight
        spec[3] = im * weight
        inverse_y(-kx * spec[3], kx * spec[2], send2c, 2)
        inverse_y(-ky * spec[3], ky * spec[2], send2c, 3)
        cube = square * mag
        inverse_y(spec[0] * cube, spec[1] * cube, send2d, 0)

    wait_bytes(recv2.at[:OWNERS], recv_sems.at[4])
    vert = inverse_x(recv2, 0)
    fields[2] = vert
    forward_x(-fields[1] * vert, send3)
    to_owners(send3, recv3, 7)

    @pl.when(is_owner)
    def _():
        to_lines(send2c, recv2c, 6)

    wait_bytes(recv2b.at[:OWNERS], recv_sems.at[5])
    fields[3] = inverse_x(recv2b, 0)

    @pl.when(is_owner)
    def _():
        kx, ky, mag, weight = wave_grids(my_p)
        wait_bytes(recv3, recv_sems.at[7])
        re, im = forward_y(recv3)
        factor = weight * mag
        spec[0] = re * factor
        spec[1] = im * factor
        inverse_y(spec[0], spec[1], send4, 0)
        to_lines(send4, recv4, 8)
        inverse_y(spec[0] * mag, spec[1] * mag, send4b, 0)
        to_lines(send4b, recv4b, 9)

    def coarsen(j):
        hi, lo = split(out_t[j])
        spec[4] = dot(hi, pairs_ref[...]) + dot(lo, pairs_ref[...])
        return spec[4, pl.ds(0, 64, stride=2), :] + spec[4, pl.ds(1, 64, stride=2), :]

    wait_bytes(recv2c.at[:OWNERS], recv_sems.at[6])
    for j in range(2):
        slope = inverse_x(recv2c, j)
        fields[5 + j] = slope
        out_t[j] = jnp.transpose(slope)
        coarse_t[j] = coarsen(j)

    def spread_with(send_sem, recv_sem, src, dst):
        for i in (5, 3, 7, 1, 4, 6, 2):
            to = (col + i) % COLS
            remote(src(to), dst, send_sem, recv_sem, row * COLS + to).start()
        pltpu.make_async_copy(src(col), dst, recv_sem).start()

    def spread(k, src, dst):
        spread_with(out_sems.at[k], out_sems.at[6 + k], src, dst)

    def spread_early(k, src, dst):
        spread_with(early_sems.at[k], early_sems.at[3 + k], src, dst)

    few = lambda k: lambda to: coarse_t.at[k, pl.ds(to * 8, 8), :]
    fine = lambda k: lambda to: out_t.at[k, pl.ds(to * LINES, LINES), :]
    my_few, my_fine = pl.ds(col * 8, 8), pl.ds(col * LINES, LINES)
    spread(2, few(0), su_tile.at[my_few, :])
    spread(3, few(1), sv_tile.at[my_few, :])
    fields[7] = inverse_x(recv2c, 2)
    fields[8] = inverse_x(recv2c, 3)

    wait_bytes(recv4.at[:OWNERS], recv_sems.at[8])
    vert_two = inverse_x(recv4, 0)
    eta = fields[1]
    fields[2] = fields[2] + vert_two
    forward_x(-eta * vert_two - 0.5 * eta * eta * fields[3], send5)
    to_owners(send5, recv5, 10)

    @pl.when(is_owner)
    def _():
        to_lines(send2d, recv2d, 12)

    pot_dx, pot_dy, height_dx, height_dy = (fields[5 + j] for j in range(4))
    stretch = 1.0 + (height_dx * height_dx + height_dy * height_dy)
    advected = -(height_dx * pot_dx + height_dy * pot_dy)
    fields[7] = stretch
    fields[8] = advected
    out_t[0] = jnp.transpose(stretch)
    spread_early(0, fine(0), stretch_out.at[my_fine, :])
    out_t[1] = jnp.transpose(advected)
    spread_early(1, fine(1), advected_out.at[my_fine, :])

    for h in halos:
        h.wait()
    wait_bytes(su_tile, out_sems.at[8])
    wait_bytes(sv_tile, out_sems.at[9])

    def derivs(q, l, top):
        b = q * LZ + l
        mid = vel[b]
        above = jnp.where(l == 0, top, vel[q * LZ + jnp.maximum(l - 1, 0)])
        below = vel[q * LZ + jnp.minimum(l + 1, LZ - 1)]
        east = jnp.where(
            lane == LANES - 1,
            pltpu.roll(high_x[...], LANES - 1 - b, axis=1),
            pltpu.roll(mid, LANES - 1, axis=1),
        )
        west = jnp.where(
            lane == 0,
            pltpu.roll(low_x[...], (LANES - b) % LANES, axis=1),
            pltpu.roll(mid, 1, axis=1),
        )
        north = jnp.where(line == 63, high_y[pl.ds(b, 1), :], pltpu.roll(mid, 63, axis=0))
        south = jnp.where(line == 0, low_y[pl.ds(b, 1), :], pltpu.roll(mid, 1, axis=0))
        lap = east + west + north + south + above + below - 6.0 * mid
        return mid, 0.5 * (east - west), 0.5 * (north - south), 0.5 * (above - below), lap

    def level(l, _):
        depth = jnp.full((64, LANES), l, jnp.int32).astype(F32) + 0.5
        drift_decay = jnp.exp(-2.0 * DECAY_RATE * depth)
        u, u_dx, u_dy, u_dz, u_lap = derivs(0, l, su_tile[...])
        v, v_dx, v_dy, v_dz, v_lap = derivs(1, l, sv_tile[...])
        w, w_dx, w_dy, w_dz, w_lap = derivs(2, l, jnp.zeros((64, LANES), F32))
        vort_x = w_dy - v_dz
        vort_y = u_dz - w_dx
        vort_z = v_dx - u_dy
        drift_u = su_tile[...] * drift_decay
        drift_v = sv_tile[...] * drift_decay

        def advance(mid, dx, dy, dz, lap, force):
            carried = u * dx + v * dy + w * dz
            return mid + FLOW_STEP * (-carried + VISCOSITY * lap + force)

        base[l] = advance(u, u_dx, u_dy, u_dz, u_lap, drift_v * vort_z)
        base[LZ + l] = advance(v, v_dx, v_dy, v_dz, v_lap, -drift_u * vort_z)
        base[2 * LZ + l] = advance(w, w_dx, w_dy, w_dz, w_lap, drift_u * vort_y - drift_v * vort_x)
        return 0

    lax.fori_loop(0, EARLY_LEVELS, level, 0)

    @pl.when(is_owner)
    def _():
        kx, ky, mag, weight = wave_grids(my_p)
        wait_bytes(recv5, recv_sems.at[10])
        re, im = forward_y(recv5)
        factor = weight * mag
        inverse_y(re * factor, im * factor, send6, 0)
        to_lines(send6, recv6, 11)

    eta = fields[1]
    pot_dx, pot_dy = fields[5], fields[6]
    out_t[2] = jnp.transpose(-GRAVITY * eta - 0.5 * (pot_dx * pot_dx + pot_dy * pot_dy))
    spread_early(2, fine(2), still_out.at[my_fine, :])
    lax.fori_loop(EARLY_LEVELS, LZ, level, 0)
    base_copy = pltpu.make_async_copy(base, base_out, load_sems.at[n_tab + 1])
    base_copy.start()
    wait_bytes(recv2d.at[:OWNERS], recv_sems.at[12])
    cube_one = inverse_x(recv2d, 0)
    wait_bytes(recv4b.at[:OWNERS], recv_sems.at[9])
    curve_two = inverse_x(recv4b, 0)
    eta = fields[1]
    fields[2] = fields[2] + eta * (fields[3] + curve_two) + 0.5 * eta * eta * cube_one

    wait_bytes(recv6.at[:OWNERS], recv_sems.at[11])
    height_rate = fields[8] + fields[7] * (fields[2] + inverse_x(recv6, 0))
    out_t[3] = jnp.transpose(height_rate)
    spread(0, fine(3), height_out.at[my_fine, :])
    out_t[4] = jnp.transpose(GRAVITY * (fields[1] + SURFACE_STEP * height_rate))
    pressure = coarsen(4)
    coarse_t[2] = pressure
    spread(5, few(2), press_out.at[pl.ds(col * 8 + 8, 8), :])

    @pl.when(col == COLS - 1)
    def _():
        for to in range(COLS):
            remote(
                coarse_t.at[2, pl.ds(to * 8, 8), :],
                press_out.at[pl.ds(0, 8), :],
                out_sems.at[12],
                out_sems.at[11],
                up_r * COLS + to,
            ).start()

    @pl.when(col == 0)
    def _():
        for to in range(COLS):
            remote(
                coarse_t.at[2, pl.ds(to * 8, 8), :],
                press_out.at[pl.ds(72, 8), :],
                out_sems.at[12],
                out_sems.at[11],
                down_r * COLS + to,
            ).start()

    east = pltpu.roll(pressure, LANES - 1, axis=1)
    east = jnp.where(lane == LANES - 1, pltpu.roll(east, 56, axis=0), east)
    west = pltpu.roll(pressure, 1, axis=1)
    west = jnp.where(lane == 0, pltpu.roll(west, 8, axis=0), west)
    coarse_t[3] = 0.5 * (east - west)
    spread(4, few(3), lx_out.at[my_few, :])

    for f in range(2):
        wait_bytes(lines.at[f, :7], send_sems.at[f])
    wait_bytes(out_t.at[3, :112, :], out_sems.at[0])
    for k in range(3):
        wait_bytes(out_t.at[k, :112, :], early_sems.at[k])
    for k in range(4):
        wait_bytes(coarse_t.at[k, :56, :], out_sems.at[2 + k])

    @pl.when((col == 0) | (col == COLS - 1))
    def _():
        wait_bytes(coarse_t.at[2], out_sems.at[12])

    owned = ((send1, 2), (send1b, 3), (send3, 7), (send5, 10))

    @pl.when(is_owner)
    def _():
        for buf, k in owned:
            wait_bytes(buf.at[: OWNERS - 1], send_sems.at[k])
        for buf, k in (
            (send2, 4),
            (send2b, 5),
            (send2c, 6),
            (send2d, 12),
            (send4, 8),
            (send4b, 9),
            (send6, 11),
        ):
            wait_bytes(buf.at[: DEVS - 1], send_sems.at[k])

    @pl.when(jnp.logical_not(is_owner))
    def _():
        for buf, k in owned:
            wait_bytes(buf.at[:OWNERS], send_sems.at[k])

    base_copy.wait()
    for k, ref in enumerate((stretch_out, advected_out, still_out)):
        wait_bytes(ref, early_sems.at[3 + k])
    for k, ref in ((0, height_out), (4, lx_out), (5, press_out)):
        wait_bytes(ref, out_sems.at[6 + k])


CHUNK = 8


def load_kernel(*refs):
    load_x, press, height, stretch, advected, still, base = refs[:7]
    out, height_out, pot_out = refs[7:10]
    stage, pot, sems = refs[10:]
    straight = [
        pltpu.make_async_copy(height, height_out, sems.at[0]),
        pltpu.make_async_copy(base.at[pl.ds(2 * LZ, LZ)], out.at[pl.ds(2 * LZ, LZ)], sems.at[1]),
    ]
    for copy in straight:
        copy.start()
    loads = (load_x[...], 0.5 * (press[9:73, :] - press[7:71, :]))
    outs = []
    for k in range(2 * LZ // CHUNK):
        for b in range(CHUNK * k, CHUNK * k + CHUNK):
            q, l = divmod(b, LZ)
            decay = float(np.exp(-DECAY_RATE * (l + 0.5)))
            stage[b] = base[b] - (FLOW_STEP * decay) * loads[q]
        part = pl.ds(CHUNK * k, CHUNK)
        outs.append(pltpu.make_async_copy(stage.at[part], out.at[part], sems.at[3 + k]))
        outs[-1].start()
    lifted = height[...] - advected[...]
    pot[...] = still[...] + 0.5 * lifted * (lifted / stretch[...])
    outs.append(pltpu.make_async_copy(pot, pot_out, sems.at[2]))
    outs[-1].start()
    for copy in straight + outs:
        copy.wait()


def in_hbm(a):
    return pltpu.with_memory_space_constraint(a, pltpu.HBM)


def local(surface_height, surface_potential, velocity):
    flow = velocity.reshape(3 * LZ, 64, LANES)
    tabs = [jnp.asarray(t) for t in tables()]
    anywhere = pl.BlockSpec(memory_space=pl.ANY)

    def shape(*dims):
        return jax.ShapeDtypeStruct(dims, F32)

    def buf(*dims):
        return VMEM(dims, F32)

    messages = []
    for kind, count in zip("oollllollol", (2, 2, 2, 2, 8, 2, 2, 2, 2, 2, 2)):
        if kind == "o":
            messages += [buf(OWN_PAD, count, LANES), buf(DEVS, count, LANES)]
        else:
            messages += [buf(DEVS, count, LANES), buf(OWN_PAD, count, LANES)]
    outs = pl.pallas_call(
        surface_kernel,
        name="surface",
        out_shape=[
            shape(128, 256),
            shape(64, LANES),
            shape(80, LANES),
            shape(3 * LZ, 64, LANES),
            shape(128, 256),
            shape(128, 256),
            shape(128, 256),
        ],
        in_specs=[anywhere] * (3 + len(tabs)),
        out_specs=[anywhere] * 7,
        scratch_shapes=[VMEM(t.shape, t.dtype) for t in tabs]
        + [buf(2, COLS, LINES, 256), buf(9, 256, LANES)]
        + messages
        + [
            buf(5, LANES, LANES),
            buf(5, LANES, 256),
            buf(4, 64, LANES),
            buf(3 * LZ, 64, LANES),
            buf(3 * LZ, 64, LANES),
            buf(2, 48, LANES),
            buf(2, 64, LANES),
            buf(48, LANES),
            buf(48, LANES),
            buf(64, LANES),
            buf(64, LANES),
            buf(64, LANES),
            buf(64, LANES),
            pltpu.SMEM((DEVS,), jnp.int32),
            pltpu.SMEM((DEVS,), jnp.int32),
            pltpu.SMEM((DEVS,), jnp.int32),
            pltpu.SemaphoreType.DMA((len(tabs) + 2,)),
            pltpu.SemaphoreType.DMA((13,)),
            pltpu.SemaphoreType.DMA((13,)),
            pltpu.SemaphoreType.DMA((13,)),
            pltpu.SemaphoreType.DMA((6,)),
            pltpu.SemaphoreType.DMA((8,)),
        ],
        compiler_params=pltpu.CompilerParams(
            collective_id=0, has_side_effects=True, vmem_limit_bytes=SURFACE_VMEM
        ),
    )(*(in_hbm(a) for a in (surface_potential, surface_height, flow, *tabs)))
    height_rate, lx, press, base, stretch, advected, still = outs
    nxt, height_rate, potential_rate = pl.pallas_call(
        load_kernel,
        name="load",
        out_shape=[shape(3 * LZ, 64, LANES), shape(128, 256), shape(128, 256)],
        in_specs=[pl.BlockSpec(memory_space=VMEM)] * 7,
        out_specs=[anywhere] * 3,
        scratch_shapes=[
            buf(2 * LZ, 64, LANES),
            buf(128, 256),
            pltpu.SemaphoreType.DMA((3 + 2 * LZ // CHUNK,)),
        ],
        compiler_params=pltpu.CompilerParams(vmem_limit_bytes=LOAD_VMEM),
    )(lx, press, height_rate, stretch, advected, still, base)
    return height_rate, potential_rate, nxt.reshape(velocity.shape)


def solution(mesh):
    specs = (P("row", "col"), P("row", "col"), P(None, None, "row", "col"))
    return jax.shard_map(local, mesh=mesh, in_specs=specs, out_specs=specs, check_vma=False)
```

```python
import functools

import jax
import jax.numpy as jnp
import numpy as np
from jax import lax
from jax.experimental import pallas as pl
from jax.experimental.pallas import tpu as pltpu
from jax.sharding import PartitionSpec as P

N = 2048
KEPT = N // 3
ROWS = 16
COLS = 8
DEVS = ROWS * COLS
LINES = 16
OWNERS = 86
OWN_PAD = 88
LANES = 128
LZ = 16
GRAVITY = 1.0
SURFACE_STEP = 0.05
FLOW_STEP = 0.5
VISCOSITY = 0.2
DECAY_RATE = 0.05
LOGICAL = pl.DeviceIdType.LOGICAL
EARLY_LEVELS = 12
SURFACE_VMEM = 20 * 1024 * 1024
LOAD_VMEM = 8 * 1024 * 1024
F32 = jnp.float32
BF16 = jnp.bfloat16
VMEM = pltpu.VMEM


def block_complex(c, s):
    return np.block([[c, -s], [s, c]])


def split_table(t):
    hi = t.astype(np.float32).astype(jnp.bfloat16)
    lo = (t - hi.astype(np.float64)).astype(np.float32).astype(jnp.bfloat16)
    return hi, lo


@functools.cache
def tables():
    def wave(a, b, n):
        ang = 2.0 * np.pi * ((a[:, None] * b[None, :]) % n) / n
        return np.cos(ang), np.sin(ang)

    r8, r16, r128, r256 = (np.arange(k) for k in (8, 16, 128, 256))
    own = np.arange(OWN_PAD)
    eye16, eye8 = np.eye(16), np.eye(8)
    c8, s8 = wave(r8, r8, 8)
    c16, s16 = wave(r16, r16, 16)
    x_first = np.concatenate([np.kron(c8, eye16), np.kron(-s8, eye16)], axis=1)
    x_last = np.concatenate([np.kron(c8, eye16), np.kron(-s8, eye16)], axis=0)
    cp, sp = wave(own, r256, 256)
    x_second = block_complex(cp, -sp)
    x_third = block_complex(cp.T, sp.T)
    c1, s1 = wave(r128, r128, 128)
    y_first = block_complex(c1, -s1)
    y_second = block_complex(np.kron(eye8, c16), np.kron(eye8, s16))
    ct, st = wave(r256, r8, N)
    x_twist = np.stack([np.repeat(ct, 16, axis=1), np.repeat(st, 16, axis=1)])
    ct, st = wave(r128, r16, N)
    y_twist = np.stack([np.tile(ct, (1, 8)), np.tile(st, (1, 8))])
    pairs = np.kron(np.eye(128), np.ones((2, 1))) * 0.25
    mats = [x_first, x_second, x_third, x_last, y_first, y_second]
    out = []
    for k, m in enumerate(mats):
        hi, lo = split_table(m)
        if k == 0:
            out.extend((np.concatenate([hi, hi], axis=0), lo))
        elif k == 3:
            out.extend((np.concatenate([hi, lo], axis=1), hi))
        else:
            out.extend((hi, lo))
    out.append(pairs.astype(np.float32).astype(jnp.bfloat16))
    out.append(x_twist.astype(np.float32))
    out.append(y_twist.astype(np.float32))
    return tuple(out)


def split(a):
    hi = a.astype(BF16)
    return hi, (a - hi.astype(F32)).astype(BF16)


def dot(a, b):
    return lax.dot_general(a, b, (((1,), (0,)), ((), ())), preferred_element_type=F32)


def left_table(table, data):
    th, tl = table
    dh, dl = split(data)
    both = dot(th, jnp.concatenate([dh, dl], axis=1))
    width = data.shape[1]
    return both[:, :width] + both[:, width:] + dot(tl, dh)


def right_table(data, table):
    th, tl = table
    dh, dl = split(data)
    return dot(dh, th) + dot(dl, th) + dot(dh, tl)


def x_forward(phys, first, second, twist):
    twice, lo = first
    dh, dl = split(phys)
    z = dot(jnp.concatenate([dh, dl], axis=1), twice) + dot(dh, lo)
    zr, zi = z[:, :LANES], z[:, LANES:]
    c, s = twist
    t = jnp.concatenate([zr * c + zi * s, zi * c - zr * s], axis=0)
    out = left_table(second, t)
    return out[:OWN_PAD], out[OWN_PAD:]


def x_inverse(re, im, third, last, twist):
    u = left_table(third, jnp.concatenate([re, im], axis=0))
    ur, ui = u[:256], u[256:]
    c, s = twist
    dh, dl = split(jnp.concatenate([ur * c - ui * s, ur * s + ui * c], axis=1))
    both, hi = last
    z = dot(dh, both)
    return z[:, :LANES] + z[:, LANES:] + dot(dl, hi)


def y_forward(re, im, first, second, twist):
    t = left_table(first, jnp.concatenate([re, im], axis=0))
    tr, ti = t[:LANES], t[LANES:]
    c, s = twist
    z = right_table(jnp.concatenate([tr * c + ti * s, ti * c - tr * s], axis=1), second)
    return z[:, :LANES], z[:, LANES:]


def y_inverse(re, im, first, second, twist):
    u = right_table(jnp.concatenate([re, -im], axis=1), second)
    ur, ui = u[:, :LANES], u[:, LANES:]
    c, s = twist
    out = left_table(first, jnp.concatenate([ur * c + ui * s, ui * c - ur * s], axis=0))
    return out[:LANES], -out[LANES:]


def wave_grids(p):
    lane = lax.broadcasted_iota(jnp.int32, (LANES, LANES), 1)
    q1 = lax.broadcasted_iota(jnp.int32, (LANES, LANES), 0)
    kx_index = lane // 16 + 8 * p
    ky_index = q1 + 128 * (lane % 16)
    ky_signed = jnp.where(ky_index < N // 2, ky_index, ky_index - N)
    unit = np.float32(2.0 * np.pi / N)
    kx = unit * kx_index.astype(F32)
    ky = unit * ky_signed.astype(F32)
    kept = (jnp.abs(ky_signed) <= KEPT) & (kx_index <= KEPT)
    fold = jnp.where(kx_index == 0, 1.0, 2.0) / float(N * N)
    weight = jnp.where(kept, fold, 0.0).astype(F32)
    return kx, ky, jnp.sqrt(kx * kx + ky * ky), weight


def get(buf, j, count):
    rows, each = buf.shape[:2]
    return buf.reshape(rows * each, LANES)[pl.ds(j, count, stride=each), :]


def put(buf, j, value):
    rows, each = buf.shape[:2]
    buf.reshape(rows * each, LANES)[pl.ds(j, value.shape[0], stride=each), :] = value


def far_first():
    hops = (0, 1, 2, 1)
    offsets = [(a, b, c) for a in range(4) for b in range(4) for c in range(4)]
    weight = (0, 1.6, 2.6, 1)
    return sorted(offsets, key=lambda o: -(weight[o[0]] + hops[o[1]] + hops[o[2]]))


def surface_kernel(*refs):
    phi_ref, eta_ref, vel_ref = refs[:3]
    n_tab = 15
    tab_in = refs[3 : 3 + n_tab]
    at = 3 + n_tab
    (
        height_out,
        lx_out,
        press_out,
        base_out,
        stretch_out,
        advected_out,
        still_out,
    ) = refs[at : at + 7]
    at += 7
    tab = refs[at : at + n_tab]
    at += n_tab
    (
        lines,
        fields,
        send1,
        recv1,
        send1b,
        recv1b,
        send2,
        recv2,
        send2b,
        recv2b,
        send2c,
        recv2c,
        send2d,
        recv2d,
        send3,
        recv3,
        send4,
        recv4,
        send4b,
        recv4b,
        send5,
        recv5,
        send6,
        recv6,
        spec,
        out_t,
        coarse_t,
        vel,
        base,
        pack_y,
        pack_x,
        low_y,
        high_y,
        low_x,
        high_x,
        su_tile,
        sv_tile,
        ids,
        own_ids,
        own_ps,
        load_sems,
        send_sems,
        recv_sems,
        out_sems,
        early_sems,
        halo_sems,
    ) = refs[at:]
    row, col = lax.axis_index("row"), lax.axis_index("col")
    me = row * COLS + col
    is_owner = me % 3 != 2
    my_p = me - me // 3

    def remote(src, dst, send_sem, recv_sem, place):
        return pltpu.make_async_remote_copy(
            src_ref=src,
            dst_ref=dst,
            send_sem=send_sem,
            recv_sem=recv_sem,
            device_id=place,
            device_id_type=LOGICAL,
        )

    def wait_bytes(ref, sem):
        pltpu.make_async_copy(ref, ref, sem).wait()

    barrier = pltpu.get_barrier_semaphore()
    for i in range(1, COLS):
        pl.semaphore_signal(
            barrier, inc=1, device_id=row * COLS + (col + i) % COLS, device_id_type=LOGICAL
        )
    for i in range(1, ROWS):
        pl.semaphore_signal(
            barrier, inc=1, device_id=((row + i) % ROWS) * COLS + col, device_id_type=LOGICAL
        )
    vel_copy = pltpu.make_async_copy(vel_ref, vel, load_sems.at[n_tab])
    vel_copy.start()
    loads = [
        pltpu.make_async_copy(src, dst, load_sems.at[k])
        for k, (src, dst) in enumerate(zip(tab_in, tab))
    ]
    for load in loads:
        load.start()

    pl.semaphore_wait(barrier, COLS + ROWS - 2)

    def rows_to_lines(f, ref):
        for i in (5, 3, 7, 1, 4, 6, 2):
            to = (col + i) % COLS
            remote(
                ref.at[pl.ds(to * LINES, LINES), :],
                lines.at[f, col],
                send_sems.at[f],
                recv_sems.at[f],
                row * COLS + to,
            ).start()
        pltpu.make_async_copy(
            ref.at[pl.ds(col * LINES, LINES), :], lines.at[f, col], recv_sems.at[f]
        ).start()

    rows_to_lines(0, phi_ref)
    rows_to_lines(1, eta_ref)

    x_at = (col % 2) * 2 + row // 8
    y_at = (row // 2) % 4
    z_at = col // 2
    x_part = [((x_at + d) % 4) % 2 * 64 + ((x_at + d) % 4) // 2 for d in range(4)]
    y_part = [((y_at + d) % 4) * 16 for d in range(4)]
    z_part = [((z_at + d) % 4) * 2 for d in range(4)]
    core = row % 2
    cores = (8 * (1 - core), 8 * core)
    slot = jnp.int32(0)
    entry = 0
    for dx, dy, dz in far_first():
        chip = x_part[dx] + y_part[dy] + z_part[dz]
        for side in cores:
            place = chip + side
            third = place // 3
            ids[entry] = place
            own_ids[slot] = place
            own_ps[slot] = place - third
            slot = slot + (place - 3 * third < 2).astype(jnp.int32)
            entry += 1

    for buf in (recv2, recv2b, recv2c, recv2d, recv4, recv4b, recv6):
        buf[OWNERS:OWN_PAD] = jnp.zeros((OWN_PAD - OWNERS,) + buf.shape[1:], F32)
    def to_owners(send, recv, k):
        def step(i, _):
            remote(
                send.at[own_ps[i]], recv.at[me], send_sems.at[k], recv_sems.at[k], own_ids[i]
            ).start()
            return 0

        lax.fori_loop(0, OWNERS - 1, step, 0, unroll=5)

        @pl.when(is_owner)
        def _():
            pltpu.make_async_copy(send.at[my_p], recv.at[me], recv_sems.at[k]).start()

        @pl.when(jnp.logical_not(is_owner))
        def _():
            step(OWNERS - 1, 0)

    def to_lines(send, recv, k):
        def step(i, _):
            other = ids[i]
            remote(
                send.at[other], recv.at[my_p], send_sems.at[k], recv_sems.at[k], other
            ).start()
            return 0

        lax.fori_loop(0, DEVS - 2, step, 0, unroll=6)
        step(DEVS - 2, 0)
        pltpu.make_async_copy(send.at[me], recv.at[my_p], recv_sems.at[k]).start()

    def tables_at(k):
        return tab[2 * k][...], tab[2 * k + 1][...]

    pairs_ref, x_twist_ref, y_twist_ref = tab[12:15]

    def forward_x(phys, send):
        re, im = x_forward(phys, tables_at(0), tables_at(1), (x_twist_ref[0], x_twist_ref[1]))
        put(send, 0, re)
        put(send, 1, im)

    def inverse_x(recv, j):
        re, im = get(recv, 2 * j, OWN_PAD), get(recv, 2 * j + 1, OWN_PAD)
        return x_inverse(re, im, tables_at(2), tables_at(3), (x_twist_ref[0], x_twist_ref[1]))

    def forward_y(recv):
        re, im = get(recv, 0, DEVS), get(recv, 1, DEVS)
        return y_forward(re, im, tables_at(4), tables_at(5), (y_twist_ref[0], y_twist_ref[1]))

    def inverse_y(re, im, send, j):
        re, im = y_inverse(re, im, tables_at(4), tables_at(5), (y_twist_ref[0], y_twist_ref[1]))
        put(send, 2 * j, re)
        put(send, 2 * j + 1, im)

    for load in loads:
        load.wait()

    wait_bytes(lines.at[0], recv_sems.at[0])
    forward_x(jnp.transpose(lines[0].reshape(LANES, 256)), send1)
    to_owners(send1, recv1, 2)
    wait_bytes(lines.at[1], recv_sems.at[1])
    fields[1] = jnp.transpose(lines[1].reshape(LANES, 256))
    forward_x(fields[1], send1b)
    to_owners(send1b, recv1b, 3)

    vel_copy.wait()
    lane = lax.broadcasted_iota(jnp.int32, (64, LANES), 1)
    line = lax.broadcasted_iota(jnp.int32, (64, LANES), 0)
    pack_y[0] = vel[:, 63, :]
    pack_y[1] = vel[:, 0, :]

    def pack(b, carry):
        last, first = carry
        value = vel[b]
        last = jnp.where(lane == b, pltpu.roll(value, b + 1, axis=1), last)
        first = jnp.where(lane == b, pltpu.roll(value, b, axis=1), first)
        return last, first

    zero = jnp.zeros((64, LANES), F32)
    last, first = lax.fori_loop(0, 3 * LZ, pack, (zero, zero), unroll=8)
    pack_x[0] = last
    pack_x[1] = first
    up_r, down_r = (row + 1) % ROWS, (row + ROWS - 1) % ROWS
    up_c, down_c = (col + 1) % COLS, (col + COLS - 1) % COLS
    halos = [
        remote(pack_y.at[0], low_y, halo_sems.at[0], halo_sems.at[4], up_r * COLS + col),
        remote(pack_y.at[1], high_y, halo_sems.at[1], halo_sems.at[5], down_r * COLS + col),
        remote(pack_x.at[0], low_x, halo_sems.at[2], halo_sems.at[6], row * COLS + up_c),
        remote(pack_x.at[1], high_x, halo_sems.at[3], halo_sems.at[7], row * COLS + down_c),
    ]
    for h in halos:
        h.start()

    @pl.when(is_owner)
    def _():
        kx, ky, mag, weight = wave_grids(my_p)
        wait_bytes(recv1, recv_sems.at[2])
        re, im = forward_y(recv1)
        spec[0] = re * weight
        spec[1] = im * weight
        inverse_y(spec[0] * mag, spec[1] * mag, send2, 0)
        to_lines(send2, recv2, 4)
        square = mag * mag
        inverse_y(spec[0] * square, spec[1] * square, send2b, 0)
        to_lines(send2b, recv2b, 5)
        inverse_y(-kx * spec[1], kx * spec[0], send2c, 0)
        inverse_y(-ky * spec[1], ky * spec[0], send2c, 1)
        wait_bytes(recv1b, recv_sems.at[3])
        re, im = forward_y(recv1b)
        spec[2] = re * weight
        spec[3] = im * weight
        inverse_y(-kx * spec[3], kx * spec[2], send2c, 2)
        inverse_y(-ky * spec[3], ky * spec[2], send2c, 3)
        cube = square * mag
        inverse_y(spec[0] * cube, spec[1] * cube, send2d, 0)

    wait_bytes(recv2.at[:OWNERS], recv_sems.at[4])
    vert = inverse_x(recv2, 0)
    fields[2] = vert
    forward_x(-fields[1] * vert, send3)
    to_owners(send3, recv3, 7)

    @pl.when(is_owner)
    def _():
        to_lines(send2c, recv2c, 6)

    wait_bytes(recv2b.at[:OWNERS], recv_sems.at[5])
    fields[3] = inverse_x(recv2b, 0)

    @pl.when(is_owner)
    def _():
        kx, ky, mag, weight = wave_grids(my_p)
        wait_bytes(recv3, recv_sems.at[7])
        re, im = forward_y(recv3)
        factor = weight * mag
        spec[0] = re * factor
        spec[1] = im * factor
        inverse_y(spec[0], spec[1], send4, 0)
        to_lines(send4, recv4, 8)
        inverse_y(spec[0] * mag, spec[1] * mag, send4b, 0)
        to_lines(send4b, recv4b, 9)

    def coarsen(j):
        hi, lo = split(out_t[j])
        spec[4] = dot(hi, pairs_ref[...]) + dot(lo, pairs_ref[...])
        return spec[4, pl.ds(0, 64, stride=2), :] + spec[4, pl.ds(1, 64, stride=2), :]

    wait_bytes(recv2c.at[:OWNERS], recv_sems.at[6])
    for j in range(2):
        slope = inverse_x(recv2c, j)
        fields[5 + j] = slope
        out_t[j] = jnp.transpose(slope)
        coarse_t[j] = coarsen(j)

    def spread_with(send_sem, recv_sem, src, dst):
        for i in (5, 3, 7, 1, 4, 6, 2):
            to = (col + i) % COLS
            remote(src(to), dst, send_sem, recv_sem, row * COLS + to).start()
        pltpu.make_async_copy(src(col), dst, recv_sem).start()

    def spread(k, src, dst):
        spread_with(out_sems.at[k], out_sems.at[6 + k], src, dst)

    def spread_early(k, src, dst):
        spread_with(early_sems.at[k], early_sems.at[3 + k], src, dst)

    few = lambda k: lambda to: coarse_t.at[k, pl.ds(to * 8, 8), :]
    fine = lambda k: lambda to: out_t.at[k, pl.ds(to * LINES, LINES), :]
    my_few, my_fine = pl.ds(col * 8, 8), pl.ds(col * LINES, LINES)
    spread(2, few(0), su_tile.at[my_few, :])
    spread(3, few(1), sv_tile.at[my_few, :])
    fields[7] = inverse_x(recv2c, 2)
    fields[8] = inverse_x(recv2c, 3)

    wait_bytes(recv4.at[:OWNERS], recv_sems.at[8])
    vert_two = inverse_x(recv4, 0)
    eta = fields[1]
    fields[2] = fields[2] + vert_two
    forward_x(-eta * vert_two - 0.5 * eta * eta * fields[3], send5)
    to_owners(send5, recv5, 10)

    @pl.when(is_owner)
    def _():
        to_lines(send2d, recv2d, 12)

    pot_dx, pot_dy, height_dx, height_dy = (fields[5 + j] for j in range(4))
    stretch = 1.0 + (height_dx * height_dx + height_dy * height_dy)
    advected = -(height_dx * pot_dx + height_dy * pot_dy)
    fields[7] = stretch
    fields[8] = advected
    out_t[0] = jnp.transpose(stretch)
    spread_early(0, fine(0), stretch_out.at[my_fine, :])
    out_t[1] = jnp.transpose(advected)
    spread_early(1, fine(1), advected_out.at[my_fine, :])

    for h in halos:
        h.wait()
    wait_bytes(su_tile, out_sems.at[8])
    wait_bytes(sv_tile, out_sems.at[9])

    def derivs(q, l, top):
        b = q * LZ + l
        mid = vel[b]
        above = jnp.where(l == 0, top, vel[q * LZ + jnp.maximum(l - 1, 0)])
        below = vel[q * LZ + jnp.minimum(l + 1, LZ - 1)]
        east = jnp.where(
            lane == LANES - 1,
            pltpu.roll(high_x[...], LANES - 1 - b, axis=1),
            pltpu.roll(mid, LANES - 1, axis=1),
        )
        west = jnp.where(
            lane == 0,
            pltpu.roll(low_x[...], (LANES - b) % LANES, axis=1),
            pltpu.roll(mid, 1, axis=1),
        )
        north = jnp.where(line == 63, high_y[pl.ds(b, 1), :], pltpu.roll(mid, 63, axis=0))
        south = jnp.where(line == 0, low_y[pl.ds(b, 1), :], pltpu.roll(mid, 1, axis=0))
        lap = east + west + north + south + above + below - 6.0 * mid
        return mid, 0.5 * (east - west), 0.5 * (north - south), 0.5 * (above - below), lap

    def level(l, _):
        depth = jnp.full((64, LANES), l, jnp.int32).astype(F32) + 0.5
        drift_decay = jnp.exp(-2.0 * DECAY_RATE * depth)
        u, u_dx, u_dy, u_dz, u_lap = derivs(0, l, su_tile[...])
        v, v_dx, v_dy, v_dz, v_lap = derivs(1, l, sv_tile[...])
        w, w_dx, w_dy, w_dz, w_lap = derivs(2, l, jnp.zeros((64, LANES), F32))
        vort_x = w_dy - v_dz
        vort_y = u_dz - w_dx
        vort_z = v_dx - u_dy
        drift_u = su_tile[...] * drift_decay
        drift_v = sv_tile[...] * drift_decay

        def advance(mid, dx, dy, dz, lap, force):
            carried = u * dx + v * dy + w * dz
            return mid + FLOW_STEP * (-carried + VISCOSITY * lap + force)

        base[l] = advance(u, u_dx, u_dy, u_dz, u_lap, drift_v * vort_z)
        base[LZ + l] = advance(v, v_dx, v_dy, v_dz, v_lap, -drift_u * vort_z)
        base[2 * LZ + l] = advance(w, w_dx, w_dy, w_dz, w_lap, drift_u * vort_y - drift_v * vort_x)
        return 0

    lax.fori_loop(0, EARLY_LEVELS, level, 0)

    @pl.when(is_owner)
    def _():
        kx, ky, mag, weight = wave_grids(my_p)
        wait_bytes(recv5, recv_sems.at[10])
        re, im = forward_y(recv5)
        factor = weight * mag
        inverse_y(re * factor, im * factor, send6, 0)
        to_lines(send6, recv6, 11)

    eta = fields[1]
    pot_dx, pot_dy = fields[5], fields[6]
    out_t[2] = jnp.transpose(-GRAVITY * eta - 0.5 * (pot_dx * pot_dx + pot_dy * pot_dy))
    spread_early(2, fine(2), still_out.at[my_fine, :])
    lax.fori_loop(EARLY_LEVELS, LZ, level, 0)
    base_copy = pltpu.make_async_copy(base, base_out, load_sems.at[n_tab + 1])
    base_copy.start()
    wait_bytes(recv2d.at[:OWNERS], recv_sems.at[12])
    cube_one = inverse_x(recv2d, 0)
    wait_bytes(recv4b.at[:OWNERS], recv_sems.at[9])
    curve_two = inverse_x(recv4b, 0)
    eta = fields[1]
    fields[2] = fields[2] + eta * (fields[3] + curve_two) + 0.5 * eta * eta * cube_one

    out_t[4] = jnp.transpose(eta)
    coarse_t[3] = coarsen(4)

    wait_bytes(recv6.at[:OWNERS], recv_sems.at[11])
    height_rate = fields[8] + fields[7] * (fields[2] + inverse_x(recv6, 0))
    out_t[3] = jnp.transpose(height_rate)
    spread(0, fine(3), height_out.at[my_fine, :])
    pressure = GRAVITY * (coarse_t[3] + SURFACE_STEP * coarsen(3))
    coarse_t[2] = pressure
    spread(5, few(2), press_out.at[pl.ds(col * 8 + 8, 8), :])

    @pl.when(col == COLS - 1)
    def _():
        for to in range(COLS):
            remote(
                coarse_t.at[2, pl.ds(to * 8, 8), :],
                press_out.at[pl.ds(0, 8), :],
                out_sems.at[12],
                out_sems.at[11],
                up_r * COLS + to,
            ).start()

    @pl.when(col == 0)
    def _():
        for to in range(COLS):
            remote(
                coarse_t.at[2, pl.ds(to * 8, 8), :],
                press_out.at[pl.ds(72, 8), :],
                out_sems.at[12],
                out_sems.at[11],
                down_r * COLS + to,
            ).start()

    east = pltpu.roll(pressure, LANES - 1, axis=1)
    east = jnp.where(lane == LANES - 1, pltpu.roll(east, 56, axis=0), east)
    west = pltpu.roll(pressure, 1, axis=1)
    west = jnp.where(lane == 0, pltpu.roll(west, 8, axis=0), west)
    coarse_t[3] = 0.5 * (east - west)
    spread(4, few(3), lx_out.at[my_few, :])

    for f in range(2):
        wait_bytes(lines.at[f, :7], send_sems.at[f])
    wait_bytes(out_t.at[3, :112, :], out_sems.at[0])
    for k in range(3):
        wait_bytes(out_t.at[k, :112, :], early_sems.at[k])
    for k in range(4):
        wait_bytes(coarse_t.at[k, :56, :], out_sems.at[2 + k])

    @pl.when((col == 0) | (col == COLS - 1))
    def _():
        wait_bytes(coarse_t.at[2], out_sems.at[12])

    owned = ((send1, 2), (send1b, 3), (send3, 7), (send5, 10))

    @pl.when(is_owner)
    def _():
        for buf, k in owned:
            wait_bytes(buf.at[: OWNERS - 1], send_sems.at[k])
        for buf, k in (
            (send2, 4),
            (send2b, 5),
            (send2c, 6),
            (send2d, 12),
            (send4, 8),
            (send4b, 9),
            (send6, 11),
        ):
            wait_bytes(buf.at[: DEVS - 1], send_sems.at[k])

    @pl.when(jnp.logical_not(is_owner))
    def _():
        for buf, k in owned:
            wait_bytes(buf.at[:OWNERS], send_sems.at[k])

    base_copy.wait()
    for k, ref in enumerate((stretch_out, advected_out, still_out)):
        wait_bytes(ref, early_sems.at[3 + k])
    for k, ref in ((0, height_out), (4, lx_out), (5, press_out)):
        wait_bytes(ref, out_sems.at[6 + k])


CHUNK = 8


def load_kernel(*refs):
    load_x, press, height, stretch, advected, still, base = refs[:7]
    out, height_out, pot_out = refs[7:10]
    stage, pot, sems = refs[10:]
    straight = [
        pltpu.make_async_copy(height, height_out, sems.at[0]),
        pltpu.make_async_copy(base.at[pl.ds(2 * LZ, LZ)], out.at[pl.ds(2 * LZ, LZ)], sems.at[1]),
    ]
    for copy in straight:
        copy.start()
    loads = (load_x[...], 0.5 * (press[9:73, :] - press[7:71, :]))
    outs = []
    for k in range(2 * LZ // CHUNK):
        for b in range(CHUNK * k, CHUNK * k + CHUNK):
            q, l = divmod(b, LZ)
            decay = float(np.exp(-DECAY_RATE * (l + 0.5)))
            stage[b] = base[b] - (FLOW_STEP * decay) * loads[q]
        part = pl.ds(CHUNK * k, CHUNK)
        outs.append(pltpu.make_async_copy(stage.at[part], out.at[part], sems.at[3 + k]))
        outs[-1].start()
    lifted = height[...] - advected[...]
    pot[...] = still[...] + 0.5 * lifted * (lifted / stretch[...])
    outs.append(pltpu.make_async_copy(pot, pot_out, sems.at[2]))
    outs[-1].start()
    for copy in straight + outs:
        copy.wait()


def in_hbm(a):
    return pltpu.with_memory_space_constraint(a, pltpu.HBM)


def local(surface_height, surface_potential, velocity):
    flow = velocity.reshape(3 * LZ, 64, LANES)
    tabs = [jnp.asarray(t) for t in tables()]
    anywhere = pl.BlockSpec(memory_space=pl.ANY)

    def shape(*dims):
        return jax.ShapeDtypeStruct(dims, F32)

    def buf(*dims):
        return VMEM(dims, F32)

    messages = []
    for kind, count in zip("oollllollol", (2, 2, 2, 2, 8, 2, 2, 2, 2, 2, 2)):
        if kind == "o":
            messages += [buf(OWN_PAD, count, LANES), buf(DEVS, count, LANES)]
        else:
            messages += [buf(DEVS, count, LANES), buf(OWN_PAD, count, LANES)]
    outs = pl.pallas_call(
        surface_kernel,
        name="surface",
        out_shape=[
            shape(128, 256),
            shape(64, LANES),
            shape(80, LANES),
            shape(3 * LZ, 64, LANES),
            shape(128, 256),
            shape(128, 256),
            shape(128, 256),
        ],
        in_specs=[anywhere] * (3 + len(tabs)),
        out_specs=[anywhere] * 7,
        scratch_shapes=[VMEM(t.shape, t.dtype) for t in tabs]
        + [buf(2, COLS, LINES, 256), buf(9, 256, LANES)]
        + messages
        + [
            buf(5, LANES, LANES),
            buf(5, LANES, 256),
            buf(4, 64, LANES),
            buf(3 * LZ, 64, LANES),
            buf(3 * LZ, 64, LANES),
            buf(2, 48, LANES),
            buf(2, 64, LANES),
            buf(48, LANES),
            buf(48, LANES),
            buf(64, LANES),
            buf(64, LANES),
            buf(64, LANES),
            buf(64, LANES),
            pltpu.SMEM((DEVS,), jnp.int32),
            pltpu.SMEM((DEVS,), jnp.int32),
            pltpu.SMEM((DEVS,), jnp.int32),
            pltpu.SemaphoreType.DMA((len(tabs) + 2,)),
            pltpu.SemaphoreType.DMA((13,)),
            pltpu.SemaphoreType.DMA((13,)),
            pltpu.SemaphoreType.DMA((13,)),
            pltpu.SemaphoreType.DMA((6,)),
            pltpu.SemaphoreType.DMA((8,)),
        ],
        compiler_params=pltpu.CompilerParams(
            collective_id=0, has_side_effects=True, vmem_limit_bytes=SURFACE_VMEM
        ),
    )(*(in_hbm(a) for a in (surface_potential, surface_height, flow, *tabs)))
    height_rate, lx, press, base, stretch, advected, still = outs
    nxt, height_rate, potential_rate = pl.pallas_call(
        load_kernel,
        name="load",
        out_shape=[shape(3 * LZ, 64, LANES), shape(128, 256), shape(128, 256)],
        in_specs=[pl.BlockSpec(memory_space=VMEM)] * 7,
        out_specs=[anywhere] * 3,
        scratch_shapes=[
            buf(2 * LZ, 64, LANES),
            buf(128, 256),
            pltpu.SemaphoreType.DMA((3 + 2 * LZ // CHUNK,)),
        ],
        compiler_params=pltpu.CompilerParams(vmem_limit_bytes=LOAD_VMEM),
    )(lx, press, height_rate, stretch, advected, still, base)
    return height_rate, potential_rate, nxt.reshape(velocity.shape)


def solution(mesh):
    specs = (P("row", "col"), P("row", "col"), P(None, None, "row", "col"))
    return jax.shard_map(local, mesh=mesh, in_specs=specs, out_specs=specs, check_vma=False)
```

```python
import functools

import jax
import jax.numpy as jnp
import numpy as np
from jax import lax
from jax.experimental import pallas as pl
from jax.experimental.pallas import tpu as pltpu
from jax.sharding import PartitionSpec as P

N = 2048
KEPT = N // 3
ROWS = 16
COLS = 8
DEVS = ROWS * COLS
LINES = 16
OWNERS = 86
OWN_PAD = 88
LANES = 128
LZ = 16
GRAVITY = 1.0
SURFACE_STEP = 0.05
FLOW_STEP = 0.5
VISCOSITY = 0.2
DECAY_RATE = 0.05
LOGICAL = pl.DeviceIdType.LOGICAL
EARLY_LEVELS = 8
SURFACE_VMEM = 20 * 1024 * 1024
LOAD_VMEM = 8 * 1024 * 1024
F32 = jnp.float32
BF16 = jnp.bfloat16
VMEM = pltpu.VMEM


def block_complex(c, s):
    return np.block([[c, -s], [s, c]])


def split_table(t):
    hi = t.astype(np.float32).astype(jnp.bfloat16)
    lo = (t - hi.astype(np.float64)).astype(np.float32).astype(jnp.bfloat16)
    return hi, lo


@functools.cache
def tables():
    def wave(a, b, n):
        ang = 2.0 * np.pi * ((a[:, None] * b[None, :]) % n) / n
        return np.cos(ang), np.sin(ang)

    r8, r16, r128, r256 = (np.arange(k) for k in (8, 16, 128, 256))
    own = np.arange(OWN_PAD)
    eye16, eye8 = np.eye(16), np.eye(8)
    c8, s8 = wave(r8, r8, 8)
    c16, s16 = wave(r16, r16, 16)
    x_first = np.concatenate([np.kron(c8, eye16), np.kron(-s8, eye16)], axis=1)
    x_last = np.concatenate([np.kron(c8, eye16), np.kron(-s8, eye16)], axis=0)
    cp, sp = wave(own, r256, 256)
    x_second = block_complex(cp, -sp)
    x_third = block_complex(cp.T, sp.T)
    c1, s1 = wave(r128, r128, 128)
    y_first = block_complex(c1, -s1)
    y_second = block_complex(np.kron(eye8, c16), np.kron(eye8, s16))
    ct, st = wave(r256, r8, N)
    x_twist = np.stack([np.repeat(ct, 16, axis=1), np.repeat(st, 16, axis=1)])
    ct, st = wave(r128, r16, N)
    y_twist = np.stack([np.tile(ct, (1, 8)), np.tile(st, (1, 8))])
    pairs = np.kron(np.eye(128), np.ones((2, 1))) * 0.25
    mats = [x_first, x_second, x_third, x_last, y_first, y_second]
    out = []
    for k, m in enumerate(mats):
        hi, lo = split_table(m)
        if k == 0:
            out.extend((np.concatenate([hi, hi], axis=0), lo))
        elif k == 3:
            out.extend((np.concatenate([hi, lo], axis=1), hi))
        else:
            out.extend((hi, lo))
    out.append(pairs.astype(np.float32).astype(jnp.bfloat16))
    out.append(x_twist.astype(np.float32))
    out.append(y_twist.astype(np.float32))
    return tuple(out)


def split(a):
    hi = a.astype(BF16)
    return hi, (a - hi.astype(F32)).astype(BF16)


def dot(a, b):
    return lax.dot_general(a, b, (((1,), (0,)), ((), ())), preferred_element_type=F32)


def left_table(table, data):
    th, tl = table
    dh, dl = split(data)
    both = dot(th, jnp.concatenate([dh, dl], axis=1))
    width = data.shape[1]
    return both[:, :width] + both[:, width:] + dot(tl, dh)


def right_table(data, table):
    th, tl = table
    dh, dl = split(data)
    return dot(dh, th) + dot(dl, th) + dot(dh, tl)


def x_forward(phys, first, second, twist):
    twice, lo = first
    dh, dl = split(phys)
    z = dot(jnp.concatenate([dh, dl], axis=1), twice) + dot(dh, lo)
    zr, zi = z[:, :LANES], z[:, LANES:]
    c, s = twist
    t = jnp.concatenate([zr * c + zi * s, zi * c - zr * s], axis=0)
    out = left_table(second, t)
    return out[:OWN_PAD], out[OWN_PAD:]


def x_inverse(re, im, third, last, twist):
    u = left_table(third, jnp.concatenate([re, im], axis=0))
    ur, ui = u[:256], u[256:]
    c, s = twist
    dh, dl = split(jnp.concatenate([ur * c - ui * s, ur * s + ui * c], axis=1))
    both, hi = last
    z = dot(dh, both)
    return z[:, :LANES] + z[:, LANES:] + dot(dl, hi)


def y_forward(re, im, first, second, twist):
    t = left_table(first, jnp.concatenate([re, im], axis=0))
    tr, ti = t[:LANES], t[LANES:]
    c, s = twist
    z = right_table(jnp.concatenate([tr * c + ti * s, ti * c - tr * s], axis=1), second)
    return z[:, :LANES], z[:, LANES:]


def y_inverse(re, im, first, second, twist):
    u = right_table(jnp.concatenate([re, -im], axis=1), second)
    ur, ui = u[:, :LANES], u[:, LANES:]
    c, s = twist
    out = left_table(first, jnp.concatenate([ur * c + ui * s, ui * c - ur * s], axis=0))
    return out[:LANES], -out[LANES:]


def wave_grids(p):
    lane = lax.broadcasted_iota(jnp.int32, (LANES, LANES), 1)
    q1 = lax.broadcasted_iota(jnp.int32, (LANES, LANES), 0)
    kx_index = lane // 16 + 8 * p
    ky_index = q1 + 128 * (lane % 16)
    ky_signed = jnp.where(ky_index < N // 2, ky_index, ky_index - N)
    unit = np.float32(2.0 * np.pi / N)
    kx = unit * kx_index.astype(F32)
    ky = unit * ky_signed.astype(F32)
    kept = (jnp.abs(ky_signed) <= KEPT) & (kx_index <= KEPT)
    fold = jnp.where(kx_index == 0, 1.0, 2.0) / float(N * N)
    weight = jnp.where(kept, fold, 0.0).astype(F32)
    return kx, ky, jnp.sqrt(kx * kx + ky * ky), weight


def get(buf, j, count):
    rows, each = buf.shape[:2]
    return buf.reshape(rows * each, LANES)[pl.ds(j, count, stride=each), :]


def put(buf, j, value):
    rows, each = buf.shape[:2]
    buf.reshape(rows * each, LANES)[pl.ds(j, value.shape[0], stride=each), :] = value


def far_first():
    hops = (0, 1, 2, 1)
    offsets = [(a, b, c) for a in range(4) for b in range(4) for c in range(4)]
    weight = (0, 1.6, 2.6, 1)
    return sorted(offsets, key=lambda o: -(weight[o[0]] + hops[o[1]] + hops[o[2]]))


def surface_kernel(*refs):
    phi_ref, eta_ref, vel_ref = refs[:3]
    n_tab = 15
    tab_in = refs[3 : 3 + n_tab]
    at = 3 + n_tab
    (
        height_out,
        lx_out,
        press_out,
        base_out,
        stretch_out,
        advected_out,
        still_out,
    ) = refs[at : at + 7]
    at += 7
    tab = refs[at : at + n_tab]
    at += n_tab
    (
        lines,
        fields,
        send1,
        recv1,
        send1b,
        recv1b,
        send2,
        recv2,
        send2b,
        recv2b,
        send2c,
        recv2c,
        send2d,
        recv2d,
        send3,
        recv3,
        send4,
        recv4,
        send4b,
        recv4b,
        send5,
        recv5,
        send6,
        recv6,
        spec,
        out_t,
        coarse_t,
        vel,
        base,
        pack_y,
        pack_x,
        low_y,
        high_y,
        low_x,
        high_x,
        su_tile,
        sv_tile,
        ids,
        own_ids,
        own_ps,
        load_sems,
        send_sems,
        recv_sems,
        out_sems,
        early_sems,
        halo_sems,
    ) = refs[at:]
    row, col = lax.axis_index("row"), lax.axis_index("col")
    me = row * COLS + col
    is_owner = me % 3 != 2
    my_p = me - me // 3

    def remote(src, dst, send_sem, recv_sem, place):
        return pltpu.make_async_remote_copy(
            src_ref=src,
            dst_ref=dst,
            send_sem=send_sem,
            recv_sem=recv_sem,
            device_id=place,
            device_id_type=LOGICAL,
        )

    def wait_bytes(ref, sem):
        pltpu.make_async_copy(ref, ref, sem).wait()

    barrier = pltpu.get_barrier_semaphore()
    for i in range(1, COLS):
        pl.semaphore_signal(
            barrier, inc=1, device_id=row * COLS + (col + i) % COLS, device_id_type=LOGICAL
        )
    for i in range(1, ROWS):
        pl.semaphore_signal(
            barrier, inc=1, device_id=((row + i) % ROWS) * COLS + col, device_id_type=LOGICAL
        )
    vel_copy = pltpu.make_async_copy(vel_ref, vel, load_sems.at[n_tab])
    vel_copy.start()
    loads = [
        pltpu.make_async_copy(src, dst, load_sems.at[k])
        for k, (src, dst) in enumerate(zip(tab_in, tab))
    ]
    for load in loads:
        load.start()

    pl.semaphore_wait(barrier, COLS + ROWS - 2)

    def rows_to_lines(f, ref):
        for i in (5, 3, 7, 1, 4, 6, 2):
            to = (col + i) % COLS
            remote(
                ref.at[pl.ds(to * LINES, LINES), :],
                lines.at[f, col],
                send_sems.at[f],
                recv_sems.at[f],
                row * COLS + to,
            ).start()
        pltpu.make_async_copy(
            ref.at[pl.ds(col * LINES, LINES), :], lines.at[f, col], recv_sems.at[f]
        ).start()

    rows_to_lines(0, phi_ref)
    rows_to_lines(1, eta_ref)

    x_at = (col % 2) * 2 + row // 8
    y_at = (row // 2) % 4
    z_at = col // 2
    x_part = [((x_at + d) % 4) % 2 * 64 + ((x_at + d) % 4) // 2 for d in range(4)]
    y_part = [((y_at + d) % 4) * 16 for d in range(4)]
    z_part = [((z_at + d) % 4) * 2 for d in range(4)]
    core = row % 2
    cores = (8 * (1 - core), 8 * core)
    slot = jnp.int32(0)
    entry = 0
    for dx, dy, dz in far_first():
        chip = x_part[dx] + y_part[dy] + z_part[dz]
        for side in cores:
            place = chip + side
            third = place // 3
            ids[entry] = place
            own_ids[slot] = place
            own_ps[slot] = place - third
            slot = slot + (place - 3 * third < 2).astype(jnp.int32)
            entry += 1

    for buf in (recv2, recv2b, recv2c, recv2d, recv4, recv4b, recv6):
        buf[OWNERS:OWN_PAD] = jnp.zeros((OWN_PAD - OWNERS,) + buf.shape[1:], F32)
    def to_owners(send, recv, k):
        def step(i, _):
            remote(
                send.at[own_ps[i]], recv.at[me], send_sems.at[k], recv_sems.at[k], own_ids[i]
            ).start()
            return 0

        lax.fori_loop(0, OWNERS - 1, step, 0, unroll=5)

        @pl.when(is_owner)
        def _():
            pltpu.make_async_copy(send.at[my_p], recv.at[me], recv_sems.at[k]).start()

        @pl.when(jnp.logical_not(is_owner))
        def _():
            step(OWNERS - 1, 0)

    def to_lines(send, recv, k):
        def step(i, _):
            other = ids[i]
            remote(
                send.at[other], recv.at[my_p], send_sems.at[k], recv_sems.at[k], other
            ).start()
            return 0

        lax.fori_loop(0, DEVS - 2, step, 0, unroll=6)
        step(DEVS - 2, 0)
        pltpu.make_async_copy(send.at[me], recv.at[my_p], recv_sems.at[k]).start()

    def tables_at(k):
        return tab[2 * k][...], tab[2 * k + 1][...]

    pairs_ref, x_twist_ref, y_twist_ref = tab[12:15]

    def forward_x(phys, send):
        re, im = x_forward(phys, tables_at(0), tables_at(1), (x_twist_ref[0], x_twist_ref[1]))
        put(send, 0, re)
        put(send, 1, im)

    def inverse_x(recv, j):
        re, im = get(recv, 2 * j, OWN_PAD), get(recv, 2 * j + 1, OWN_PAD)
        return x_inverse(re, im, tables_at(2), tables_at(3), (x_twist_ref[0], x_twist_ref[1]))

    def forward_y(recv):
        re, im = get(recv, 0, DEVS), get(recv, 1, DEVS)
        return y_forward(re, im, tables_at(4), tables_at(5), (y_twist_ref[0], y_twist_ref[1]))

    def inverse_y(re, im, send, j):
        re, im = y_inverse(re, im, tables_at(4), tables_at(5), (y_twist_ref[0], y_twist_ref[1]))
        put(send, 2 * j, re)
        put(send, 2 * j + 1, im)

    for load in loads:
        load.wait()

    wait_bytes(lines.at[0], recv_sems.at[0])
    forward_x(jnp.transpose(lines[0].reshape(LANES, 256)), send1)
    to_owners(send1, recv1, 2)
    wait_bytes(lines.at[1], recv_sems.at[1])
    fields[1] = jnp.transpose(lines[1].reshape(LANES, 256))
    forward_x(fields[1], send1b)
    to_owners(send1b, recv1b, 3)

    vel_copy.wait()
    lane = lax.broadcasted_iota(jnp.int32, (64, LANES), 1)
    line = lax.broadcasted_iota(jnp.int32, (64, LANES), 0)
    pack_y[0] = vel[:, 63, :]
    pack_y[1] = vel[:, 0, :]

    def pack(b, carry):
        last, first = carry
        value = vel[b]
        last = jnp.where(lane == b, pltpu.roll(value, b + 1, axis=1), last)
        first = jnp.where(lane == b, pltpu.roll(value, b, axis=1), first)
        return last, first

    zero = jnp.zeros((64, LANES), F32)
    last, first = lax.fori_loop(0, 3 * LZ, pack, (zero, zero), unroll=8)
    pack_x[0] = last
    pack_x[1] = first
    up_r, down_r = (row + 1) % ROWS, (row + ROWS - 1) % ROWS
    up_c, down_c = (col + 1) % COLS, (col + COLS - 1) % COLS
    halos = [
        remote(pack_y.at[0], low_y, halo_sems.at[0], halo_sems.at[4], up_r * COLS + col),
        remote(pack_y.at[1], high_y, halo_sems.at[1], halo_sems.at[5], down_r * COLS + col),
        remote(pack_x.at[0], low_x, halo_sems.at[2], halo_sems.at[6], row * COLS + up_c),
        remote(pack_x.at[1], high_x, halo_sems.at[3], halo_sems.at[7], row * COLS + down_c),
    ]
    for h in halos:
        h.start()

    @pl.when(is_owner)
    def _():
        kx, ky, mag, weight = wave_grids(my_p)
        wait_bytes(recv1, recv_sems.at[2])
        re, im = forward_y(recv1)
        spec[0] = re * weight
        spec[1] = im * weight
        inverse_y(spec[0] * mag, spec[1] * mag, send2, 0)
        to_lines(send2, recv2, 4)
        square = mag * mag
        inverse_y(spec[0] * square, spec[1] * square, send2b, 0)
        to_lines(send2b, recv2b, 5)
        inverse_y(-kx * spec[1], kx * spec[0], send2c, 0)
        inverse_y(-ky * spec[1], ky * spec[0], send2c, 1)
        wait_bytes(recv1b, recv_sems.at[3])
        re, im = forward_y(recv1b)
        spec[2] = re * weight
        spec[3] = im * weight
        inverse_y(-kx * spec[3], kx * spec[2], send2c, 2)
        inverse_y(-ky * spec[3], ky * spec[2], send2c, 3)
        cube = square * mag
        inverse_y(spec[0] * cube, spec[1] * cube, send2d, 0)

    wait_bytes(recv2.at[:OWNERS], recv_sems.at[4])
    vert = inverse_x(recv2, 0)
    fields[2] = vert
    forward_x(-fields[1] * vert, send3)
    to_owners(send3, recv3, 7)

    @pl.when(is_owner)
    def _():
        to_lines(send2c, recv2c, 6)

    wait_bytes(recv2b.at[:OWNERS], recv_sems.at[5])
    fields[3] = inverse_x(recv2b, 0)

    @pl.when(is_owner)
    def _():
        kx, ky, mag, weight = wave_grids(my_p)
        wait_bytes(recv3, recv_sems.at[7])
        re, im = forward_y(recv3)
        factor = weight * mag
        spec[0] = re * factor
        spec[1] = im * factor
        inverse_y(spec[0], spec[1], send4, 0)
        to_lines(send4, recv4, 8)
        inverse_y(spec[0] * mag, spec[1] * mag, send4b, 0)
        to_lines(send4b, recv4b, 9)

    def coarsen(j):
        hi, lo = split(out_t[j])
        spec[4] = dot(hi, pairs_ref[...]) + dot(lo, pairs_ref[...])
        return spec[4, pl.ds(0, 64, stride=2), :] + spec[4, pl.ds(1, 64, stride=2), :]

    wait_bytes(recv2c.at[:OWNERS], recv_sems.at[6])
    for j in range(2):
        slope = inverse_x(recv2c, j)
        fields[5 + j] = slope
        out_t[j] = jnp.transpose(slope)
        coarse_t[j] = coarsen(j)

    def spread_with(send_sem, recv_sem, src, dst):
        for i in (5, 3, 7, 1, 4, 6, 2):
            to = (col + i) % COLS
            remote(src(to), dst, send_sem, recv_sem, row * COLS + to).start()
        pltpu.make_async_copy(src(col), dst, recv_sem).start()

    def spread(k, src, dst):
        spread_with(out_sems.at[k], out_sems.at[6 + k], src, dst)

    def spread_early(k, src, dst):
        spread_with(early_sems.at[k], early_sems.at[3 + k], src, dst)

    few = lambda k: lambda to: coarse_t.at[k, pl.ds(to * 8, 8), :]
    fine = lambda k: lambda to: out_t.at[k, pl.ds(to * LINES, LINES), :]
    my_few, my_fine = pl.ds(col * 8, 8), pl.ds(col * LINES, LINES)
    spread(2, few(0), su_tile.at[my_few, :])
    spread(3, few(1), sv_tile.at[my_few, :])

    wait_bytes(recv4.at[:OWNERS], recv_sems.at[8])
    vert_two = inverse_x(recv4, 0)
    eta = fields[1]
    fields[2] = fields[2] + vert_two
    forward_x(-eta * vert_two - 0.5 * eta * eta * fields[3], send5)
    to_owners(send5, recv5, 10)

    @pl.when(is_owner)
    def _():
        to_lines(send2d, recv2d, 12)

    pot_dx, pot_dy = fields[5], fields[6]
    height_dx, height_dy = inverse_x(recv2c, 2), inverse_x(recv2c, 3)
    stretch = 1.0 + (height_dx * height_dx + height_dy * height_dy)
    advected = -(height_dx * pot_dx + height_dy * pot_dy)
    fields[7] = stretch
    fields[8] = advected
    out_t[0] = jnp.transpose(stretch)
    spread_early(0, fine(0), stretch_out.at[my_fine, :])
    out_t[1] = jnp.transpose(advected)
    spread_early(1, fine(1), advected_out.at[my_fine, :])

    for h in halos:
        h.wait()
    wait_bytes(su_tile, out_sems.at[8])
    wait_bytes(sv_tile, out_sems.at[9])

    def derivs(q, l, top):
        b = q * LZ + l
        mid = vel[b]
        above = jnp.where(l == 0, top, vel[q * LZ + jnp.maximum(l - 1, 0)])
        below = vel[q * LZ + jnp.minimum(l + 1, LZ - 1)]
        east = jnp.where(
            lane == LANES - 1,
            pltpu.roll(high_x[...], LANES - 1 - b, axis=1),
            pltpu.roll(mid, LANES - 1, axis=1),
        )
        west = jnp.where(
            lane == 0,
            pltpu.roll(low_x[...], (LANES - b) % LANES, axis=1),
            pltpu.roll(mid, 1, axis=1),
        )
        north = jnp.where(line == 63, high_y[pl.ds(b, 1), :], pltpu.roll(mid, 63, axis=0))
        south = jnp.where(line == 0, low_y[pl.ds(b, 1), :], pltpu.roll(mid, 1, axis=0))
        lap = east + west + north + south + above + below - 6.0 * mid
        return mid, 0.5 * (east - west), 0.5 * (north - south), 0.5 * (above - below), lap

    def level(l, _):
        depth = jnp.full((64, LANES), l, jnp.int32).astype(F32) + 0.5
        drift_decay = jnp.exp(-2.0 * DECAY_RATE * depth)
        u, u_dx, u_dy, u_dz, u_lap = derivs(0, l, su_tile[...])
        v, v_dx, v_dy, v_dz, v_lap = derivs(1, l, sv_tile[...])
        w, w_dx, w_dy, w_dz, w_lap = derivs(2, l, jnp.zeros((64, LANES), F32))
        vort_x = w_dy - v_dz
        vort_y = u_dz - w_dx
        vort_z = v_dx - u_dy
        drift_u = su_tile[...] * drift_decay
        drift_v = sv_tile[...] * drift_decay

        def advance(mid, dx, dy, dz, lap, force):
            carried = u * dx + v * dy + w * dz
            return mid + FLOW_STEP * (-carried + VISCOSITY * lap + force)

        base[l] = advance(u, u_dx, u_dy, u_dz, u_lap, drift_v * vort_z)
        base[LZ + l] = advance(v, v_dx, v_dy, v_dz, v_lap, -drift_u * vort_z)
        base[2 * LZ + l] = advance(w, w_dx, w_dy, w_dz, w_lap, drift_u * vort_y - drift_v * vort_x)
        return 0

    lax.fori_loop(0, EARLY_LEVELS, level, 0)

    @pl.when(is_owner)
    def _():
        kx, ky, mag, weight = wave_grids(my_p)
        wait_bytes(recv5, recv_sems.at[10])
        re, im = forward_y(recv5)
        factor = weight * mag
        inverse_y(re * factor, im * factor, send6, 0)
        to_lines(send6, recv6, 11)

    eta = fields[1]
    pot_dx, pot_dy = fields[5], fields[6]
    out_t[2] = jnp.transpose(-GRAVITY * eta - 0.5 * (pot_dx * pot_dx + pot_dy * pot_dy))
    spread_early(2, fine(2), still_out.at[my_fine, :])
    lax.fori_loop(EARLY_LEVELS, LZ, level, 0)
    base_copy = pltpu.make_async_copy(base, base_out, load_sems.at[n_tab + 1])
    base_copy.start()
    wait_bytes(recv2d.at[:OWNERS], recv_sems.at[12])
    cube_one = inverse_x(recv2d, 0)
    wait_bytes(recv4b.at[:OWNERS], recv_sems.at[9])
    curve_two = inverse_x(recv4b, 0)
    eta = fields[1]
    fields[2] = fields[2] + eta * (fields[3] + curve_two) + 0.5 * eta * eta * cube_one

    out_t[4] = jnp.transpose(eta)
    coarse_t[3] = coarsen(4)

    wait_bytes(recv6.at[:OWNERS], recv_sems.at[11])
    height_rate = fields[8] + fields[7] * (fields[2] + inverse_x(recv6, 0))
    out_t[3] = jnp.transpose(height_rate)
    spread(0, fine(3), height_out.at[my_fine, :])
    pressure = GRAVITY * (coarse_t[3] + SURFACE_STEP * coarsen(3))
    coarse_t[2] = pressure
    spread(5, few(2), press_out.at[pl.ds(col * 8 + 8, 8), :])

    @pl.when(col == COLS - 1)
    def _():
        for to in range(COLS):
            remote(
                coarse_t.at[2, pl.ds(to * 8, 8), :],
                press_out.at[pl.ds(0, 8), :],
                out_sems.at[12],
                out_sems.at[11],
                up_r * COLS + to,
            ).start()

    @pl.when(col == 0)
    def _():
        for to in range(COLS):
            remote(
                coarse_t.at[2, pl.ds(to * 8, 8), :],
                press_out.at[pl.ds(72, 8), :],
                out_sems.at[12],
                out_sems.at[11],
                down_r * COLS + to,
            ).start()

    east = pltpu.roll(pressure, LANES - 1, axis=1)
    east = jnp.where(lane == LANES - 1, pltpu.roll(east, 56, axis=0), east)
    west = pltpu.roll(pressure, 1, axis=1)
    west = jnp.where(lane == 0, pltpu.roll(west, 8, axis=0), west)
    coarse_t[3] = 0.5 * (east - west)
    spread(4, few(3), lx_out.at[my_few, :])

    for f in range(2):
        wait_bytes(lines.at[f, :7], send_sems.at[f])
    wait_bytes(out_t.at[3, :112, :], out_sems.at[0])
    for k in range(3):
        wait_bytes(out_t.at[k, :112, :], early_sems.at[k])
    for k in range(4):
        wait_bytes(coarse_t.at[k, :56, :], out_sems.at[2 + k])

    @pl.when((col == 0) | (col == COLS - 1))
    def _():
        wait_bytes(coarse_t.at[2], out_sems.at[12])

    owned = ((send1, 2), (send1b, 3), (send3, 7), (send5, 10))

    @pl.when(is_owner)
    def _():
        for buf, k in owned:
            wait_bytes(buf.at[: OWNERS - 1], send_sems.at[k])
        for buf, k in (
            (send2, 4),
            (send2b, 5),
            (send2c, 6),
            (send2d, 12),
            (send4, 8),
            (send4b, 9),
            (send6, 11),
        ):
            wait_bytes(buf.at[: DEVS - 1], send_sems.at[k])

    @pl.when(jnp.logical_not(is_owner))
    def _():
        for buf, k in owned:
            wait_bytes(buf.at[:OWNERS], send_sems.at[k])

    base_copy.wait()
    for k, ref in enumerate((stretch_out, advected_out, still_out)):
        wait_bytes(ref, early_sems.at[3 + k])
    for k, ref in ((0, height_out), (4, lx_out), (5, press_out)):
        wait_bytes(ref, out_sems.at[6 + k])


CHUNK = 8


def load_kernel(*refs):
    load_x, press, height, stretch, advected, still, base = refs[:7]
    out, height_out, pot_out = refs[7:10]
    stage, pot, sems = refs[10:]
    straight = [
        pltpu.make_async_copy(height, height_out, sems.at[0]),
        pltpu.make_async_copy(base.at[pl.ds(2 * LZ, LZ)], out.at[pl.ds(2 * LZ, LZ)], sems.at[1]),
    ]
    for copy in straight:
        copy.start()
    loads = (load_x[...], 0.5 * (press[9:73, :] - press[7:71, :]))
    outs = []
    for k in range(2 * LZ // CHUNK):
        for b in range(CHUNK * k, CHUNK * k + CHUNK):
            q, l = divmod(b, LZ)
            decay = float(np.exp(-DECAY_RATE * (l + 0.5)))
            stage[b] = base[b] - (FLOW_STEP * decay) * loads[q]
        part = pl.ds(CHUNK * k, CHUNK)
        outs.append(pltpu.make_async_copy(stage.at[part], out.at[part], sems.at[3 + k]))
        outs[-1].start()
    lifted = height[...] - advected[...]
    pot[...] = still[...] + 0.5 * lifted * (lifted / stretch[...])
    outs.append(pltpu.make_async_copy(pot, pot_out, sems.at[2]))
    outs[-1].start()
    for copy in straight + outs:
        copy.wait()


def in_hbm(a):
    return pltpu.with_memory_space_constraint(a, pltpu.HBM)


def local(surface_height, surface_potential, velocity):
    flow = velocity.reshape(3 * LZ, 64, LANES)
    tabs = [jnp.asarray(t) for t in tables()]
    anywhere = pl.BlockSpec(memory_space=pl.ANY)

    def shape(*dims):
        return jax.ShapeDtypeStruct(dims, F32)

    def buf(*dims):
        return VMEM(dims, F32)

    messages = []
    for kind, count in zip("oollllollol", (2, 2, 2, 2, 8, 2, 2, 2, 2, 2, 2)):
        if kind == "o":
            messages += [buf(OWN_PAD, count, LANES), buf(DEVS, count, LANES)]
        else:
            messages += [buf(DEVS, count, LANES), buf(OWN_PAD, count, LANES)]
    outs = pl.pallas_call(
        surface_kernel,
        name="surface",
        out_shape=[
            shape(128, 256),
            shape(64, LANES),
            shape(80, LANES),
            shape(3 * LZ, 64, LANES),
            shape(128, 256),
            shape(128, 256),
            shape(128, 256),
        ],
        in_specs=[anywhere] * (3 + len(tabs)),
        out_specs=[anywhere] * 7,
        scratch_shapes=[VMEM(t.shape, t.dtype) for t in tabs]
        + [buf(2, COLS, LINES, 256), buf(9, 256, LANES)]
        + messages
        + [
            buf(5, LANES, LANES),
            buf(5, LANES, 256),
            buf(4, 64, LANES),
            buf(3 * LZ, 64, LANES),
            buf(3 * LZ, 64, LANES),
            buf(2, 48, LANES),
            buf(2, 64, LANES),
            buf(48, LANES),
            buf(48, LANES),
            buf(64, LANES),
            buf(64, LANES),
            buf(64, LANES),
            buf(64, LANES),
            pltpu.SMEM((DEVS,), jnp.int32),
            pltpu.SMEM((DEVS,), jnp.int32),
            pltpu.SMEM((DEVS,), jnp.int32),
            pltpu.SemaphoreType.DMA((len(tabs) + 2,)),
            pltpu.SemaphoreType.DMA((13,)),
            pltpu.SemaphoreType.DMA((13,)),
            pltpu.SemaphoreType.DMA((13,)),
            pltpu.SemaphoreType.DMA((6,)),
            pltpu.SemaphoreType.DMA((8,)),
        ],
        compiler_params=pltpu.CompilerParams(
            collective_id=0, has_side_effects=True, vmem_limit_bytes=SURFACE_VMEM
        ),
    )(*(in_hbm(a) for a in (surface_potential, surface_height, flow, *tabs)))
    height_rate, lx, press, base, stretch, advected, still = outs
    nxt, height_rate, potential_rate = pl.pallas_call(
        load_kernel,
        name="load",
        out_shape=[shape(3 * LZ, 64, LANES), shape(128, 256), shape(128, 256)],
        in_specs=[pl.BlockSpec(memory_space=VMEM)] * 7,
        out_specs=[anywhere] * 3,
        scratch_shapes=[
            buf(2 * LZ, 64, LANES),
            buf(128, 256),
            pltpu.SemaphoreType.DMA((3 + 2 * LZ // CHUNK,)),
        ],
        compiler_params=pltpu.CompilerParams(vmem_limit_bytes=LOAD_VMEM),
    )(lx, press, height_rate, stretch, advected, still, base)
    return height_rate, potential_rate, nxt.reshape(velocity.shape)


def solution(mesh):
    specs = (P("row", "col"), P("row", "col"), P(None, None, "row", "col"))
    return jax.shard_map(local, mesh=mesh, in_specs=specs, out_specs=specs, check_vma=False)
```

```python
import functools

import jax
import jax.numpy as jnp
import numpy as np
from jax import lax
from jax.experimental import pallas as pl
from jax.experimental.pallas import tpu as pltpu
from jax.sharding import PartitionSpec as P

N = 2048
KEPT = N // 3
ROWS = 16
COLS = 8
DEVS = ROWS * COLS
LINES = 16
OWNERS = 86
OWN_PAD = 88
LANES = 128
LZ = 16
GRAVITY = 1.0
SURFACE_STEP = 0.05
FLOW_STEP = 0.5
VISCOSITY = 0.2
DECAY_RATE = 0.05
LOGICAL = pl.DeviceIdType.LOGICAL
EARLY_LEVELS = 8
SURFACE_VMEM = 20 * 1024 * 1024
LOAD_VMEM = 8 * 1024 * 1024
F32 = jnp.float32
BF16 = jnp.bfloat16
VMEM = pltpu.VMEM


def block_complex(c, s):
    return np.block([[c, -s], [s, c]])


def split_table(t):
    hi = t.astype(np.float32).astype(jnp.bfloat16)
    lo = (t - hi.astype(np.float64)).astype(np.float32).astype(jnp.bfloat16)
    return hi, lo


@functools.cache
def tables():
    def wave(a, b, n):
        ang = 2.0 * np.pi * ((a[:, None] * b[None, :]) % n) / n
        return np.cos(ang), np.sin(ang)

    r8, r16, r128, r256 = (np.arange(k) for k in (8, 16, 128, 256))
    own = np.arange(OWN_PAD)
    eye16, eye8 = np.eye(16), np.eye(8)
    c8, s8 = wave(r8, r8, 8)
    c16, s16 = wave(r16, r16, 16)
    x_first = np.concatenate([np.kron(c8, eye16), np.kron(-s8, eye16)], axis=1)
    x_last = np.concatenate([np.kron(c8, eye16), np.kron(-s8, eye16)], axis=0)
    cp, sp = wave(own, r256, 256)
    x_second = block_complex(cp, -sp)
    x_third = block_complex(cp.T, sp.T)
    c1, s1 = wave(r128, r128, 128)
    y_first = block_complex(c1, -s1)
    y_second = block_complex(np.kron(eye8, c16), np.kron(eye8, s16))
    ct, st = wave(r256, r8, N)
    x_twist = np.stack([np.repeat(ct, 16, axis=1), np.repeat(st, 16, axis=1)])
    ct, st = wave(r128, r16, N)
    y_twist = np.stack([np.tile(ct, (1, 8)), np.tile(st, (1, 8))])
    pairs = np.kron(np.eye(128), np.ones((2, 1))) * 0.25
    mats = [x_first, x_second, x_third, x_last, y_first, y_second]
    out = []
    for k, m in enumerate(mats):
        hi, lo = split_table(m)
        if k == 0:
            out.extend((np.concatenate([hi, hi], axis=0), lo))
        elif k == 3:
            out.extend((np.concatenate([hi, lo], axis=1), hi))
        else:
            out.extend((hi, lo))
    out.append(pairs.astype(np.float32).astype(jnp.bfloat16))
    out.append(x_twist.astype(np.float32))
    out.append(y_twist.astype(np.float32))
    return tuple(out)


def split(a):
    hi = a.astype(BF16)
    return hi, (a - hi.astype(F32)).astype(BF16)


def dot(a, b):
    return lax.dot_general(a, b, (((1,), (0,)), ((), ())), preferred_element_type=F32)


def left_table(table, data):
    th, tl = table
    dh, dl = split(data)
    both = dot(th, jnp.concatenate([dh, dl], axis=1))
    width = data.shape[1]
    return both[:, :width] + both[:, width:] + dot(tl, dh)


def right_table(data, table):
    th, tl = table
    dh, dl = split(data)
    return dot(dh, th) + dot(dl, th) + dot(dh, tl)


def x_forward(phys, first, second, twist):
    twice, lo = first
    dh, dl = split(phys)
    z = dot(jnp.concatenate([dh, dl], axis=1), twice) + dot(dh, lo)
    zr, zi = z[:, :LANES], z[:, LANES:]
    c, s = twist
    t = jnp.concatenate([zr * c + zi * s, zi * c - zr * s], axis=0)
    out = left_table(second, t)
    return out[:OWN_PAD], out[OWN_PAD:]


def x_inverse(re, im, third, last, twist):
    u = left_table(third, jnp.concatenate([re, im], axis=0))
    ur, ui = u[:256], u[256:]
    c, s = twist
    dh, dl = split(jnp.concatenate([ur * c - ui * s, ur * s + ui * c], axis=1))
    both, hi = last
    z = dot(dh, both)
    return z[:, :LANES] + z[:, LANES:] + dot(dl, hi)


def y_forward(re, im, first, second, twist):
    t = left_table(first, jnp.concatenate([re, im], axis=0))
    tr, ti = t[:LANES], t[LANES:]
    c, s = twist
    z = right_table(jnp.concatenate([tr * c + ti * s, ti * c - tr * s], axis=1), second)
    return z[:, :LANES], z[:, LANES:]


def y_inverse(re, im, first, second, twist):
    u = right_table(jnp.concatenate([re, -im], axis=1), second)
    ur, ui = u[:, :LANES], u[:, LANES:]
    c, s = twist
    out = left_table(first, jnp.concatenate([ur * c + ui * s, ui * c - ur * s], axis=0))
    return out[:LANES], -out[LANES:]


def wave_grids(p):
    lane = lax.broadcasted_iota(jnp.int32, (LANES, LANES), 1)
    q1 = lax.broadcasted_iota(jnp.int32, (LANES, LANES), 0)
    kx_index = lane // 16 + 8 * p
    ky_index = q1 + 128 * (lane % 16)
    ky_signed = jnp.where(ky_index < N // 2, ky_index, ky_index - N)
    unit = np.float32(2.0 * np.pi / N)
    kx = unit * kx_index.astype(F32)
    ky = unit * ky_signed.astype(F32)
    kept = (jnp.abs(ky_signed) <= KEPT) & (kx_index <= KEPT)
    fold = jnp.where(kx_index == 0, 1.0, 2.0) / float(N * N)
    weight = jnp.where(kept, fold, 0.0).astype(F32)
    return kx, ky, jnp.sqrt(kx * kx + ky * ky), weight


def get(buf, j, count):
    rows, each = buf.shape[:2]
    return buf.reshape(rows * each, LANES)[pl.ds(j, count, stride=each), :]


def put(buf, j, value):
    rows, each = buf.shape[:2]
    buf.reshape(rows * each, LANES)[pl.ds(j, value.shape[0], stride=each), :] = value


def far_first():
    hops = (0, 1, 2, 1)
    offsets = [(a, b, c) for a in range(4) for b in range(4) for c in range(4)]
    weight = (0, 1.6, 2.6, 1)
    return sorted(offsets, key=lambda o: -(weight[o[0]] + hops[o[1]] + hops[o[2]]))


def surface_kernel(*refs):
    phi_ref, eta_ref, vel_ref = refs[:3]
    n_tab = 15
    tab_in = refs[3 : 3 + n_tab]
    at = 3 + n_tab
    (
        height_out,
        lx_out,
        press_out,
        base_out,
        stretch_out,
        advected_out,
        still_out,
    ) = refs[at : at + 7]
    at += 7
    tab = refs[at : at + n_tab]
    at += n_tab
    (
        lines,
        fields,
        send1,
        recv1,
        send1b,
        recv1b,
        send2,
        recv2,
        send2b,
        recv2b,
        send2c,
        recv2c,
        send2d,
        recv2d,
        send3,
        recv3,
        send4,
        recv4,
        send4b,
        recv4b,
        send5,
        recv5,
        send6,
        recv6,
        spec,
        out_t,
        coarse_t,
        vel,
        base,
        pack_y,
        pack_x,
        low_y,
        high_y,
        low_x,
        high_x,
        su_tile,
        sv_tile,
        ids,
        own_ids,
        own_ps,
        load_sems,
        send_sems,
        recv_sems,
        out_sems,
        early_sems,
        halo_sems,
    ) = refs[at:]
    row, col = lax.axis_index("row"), lax.axis_index("col")
    me = row * COLS + col
    is_owner = me % 3 != 2
    my_p = me - me // 3

    def remote(src, dst, send_sem, recv_sem, place):
        return pltpu.make_async_remote_copy(
            src_ref=src,
            dst_ref=dst,
            send_sem=send_sem,
            recv_sem=recv_sem,
            device_id=place,
            device_id_type=LOGICAL,
        )

    def wait_bytes(ref, sem):
        pltpu.make_async_copy(ref, ref, sem).wait()

    barrier = pltpu.get_barrier_semaphore()
    for i in range(1, COLS):
        pl.semaphore_signal(
            barrier, inc=1, device_id=row * COLS + (col + i) % COLS, device_id_type=LOGICAL
        )
    for i in range(1, ROWS):
        pl.semaphore_signal(
            barrier, inc=1, device_id=((row + i) % ROWS) * COLS + col, device_id_type=LOGICAL
        )
    vel_copy = pltpu.make_async_copy(vel_ref, vel, load_sems.at[n_tab])
    vel_copy.start()
    loads = [
        pltpu.make_async_copy(src, dst, load_sems.at[k])
        for k, (src, dst) in enumerate(zip(tab_in, tab))
    ]
    for load in loads:
        load.start()

    pl.semaphore_wait(barrier, COLS + ROWS - 2)

    def rows_to_lines(f, ref):
        for i in (5, 3, 7, 1, 4, 6, 2):
            to = (col + i) % COLS
            remote(
                ref.at[pl.ds(to * LINES, LINES), :],
                lines.at[f, col],
                send_sems.at[f],
                recv_sems.at[f],
                row * COLS + to,
            ).start()
        pltpu.make_async_copy(
            ref.at[pl.ds(col * LINES, LINES), :], lines.at[f, col], recv_sems.at[f]
        ).start()

    rows_to_lines(0, phi_ref)
    rows_to_lines(1, eta_ref)

    x_at = (col % 2) * 2 + row // 8
    y_at = (row // 2) % 4
    z_at = col // 2
    x_part = [((x_at + d) % 4) % 2 * 64 + ((x_at + d) % 4) // 2 for d in range(4)]
    y_part = [((y_at + d) % 4) * 16 for d in range(4)]
    z_part = [((z_at + d) % 4) * 2 for d in range(4)]
    core = row % 2
    cores = (8 * (1 - core), 8 * core)
    slot = jnp.int32(0)
    entry = 0
    for dx, dy, dz in far_first():
        chip = x_part[dx] + y_part[dy] + z_part[dz]
        for side in cores:
            place = chip + side
            third = place // 3
            ids[entry] = place
            own_ids[slot] = place
            own_ps[slot] = place - third
            slot = slot + (place - 3 * third < 2).astype(jnp.int32)
            entry += 1

    for buf in (recv2, recv2b, recv2c, recv2d, recv4, recv4b, recv6):
        buf[OWNERS:OWN_PAD] = jnp.zeros((OWN_PAD - OWNERS,) + buf.shape[1:], F32)
    def to_owners(send, recv, k):
        def step(i, _):
            remote(
                send.at[own_ps[i]], recv.at[me], send_sems.at[k], recv_sems.at[k], own_ids[i]
            ).start()
            return 0

        lax.fori_loop(0, OWNERS - 1, step, 0, unroll=17)

        @pl.when(is_owner)
        def _():
            pltpu.make_async_copy(send.at[my_p], recv.at[me], recv_sems.at[k]).start()

        @pl.when(jnp.logical_not(is_owner))
        def _():
            step(OWNERS - 1, 0)

    def to_lines(send, recv, k):
        def step(i, _):
            other = ids[i]
            remote(
                send.at[other], recv.at[my_p], send_sems.at[k], recv_sems.at[k], other
            ).start()
            return 0

        lax.fori_loop(0, DEVS - 2, step, 0, unroll=18)
        step(DEVS - 2, 0)
        pltpu.make_async_copy(send.at[me], recv.at[my_p], recv_sems.at[k]).start()

    def tables_at(k):
        return tab[2 * k][...], tab[2 * k + 1][...]

    pairs_ref, x_twist_ref, y_twist_ref = tab[12:15]

    def forward_x(phys, send):
        re, im = x_forward(phys, tables_at(0), tables_at(1), (x_twist_ref[0], x_twist_ref[1]))
        put(send, 0, re)
        put(send, 1, im)

    def inverse_x(recv, j):
        re, im = get(recv, 2 * j, OWN_PAD), get(recv, 2 * j + 1, OWN_PAD)
        return x_inverse(re, im, tables_at(2), tables_at(3), (x_twist_ref[0], x_twist_ref[1]))

    def forward_y(recv):
        re, im = get(recv, 0, DEVS), get(recv, 1, DEVS)
        return y_forward(re, im, tables_at(4), tables_at(5), (y_twist_ref[0], y_twist_ref[1]))

    def inverse_y(re, im, send, j):
        re, im = y_inverse(re, im, tables_at(4), tables_at(5), (y_twist_ref[0], y_twist_ref[1]))
        put(send, 2 * j, re)
        put(send, 2 * j + 1, im)

    for load in loads:
        load.wait()

    wait_bytes(lines.at[0], recv_sems.at[0])
    forward_x(jnp.transpose(lines[0].reshape(LANES, 256)), send1)
    to_owners(send1, recv1, 2)
    wait_bytes(lines.at[1], recv_sems.at[1])
    fields[1] = jnp.transpose(lines[1].reshape(LANES, 256))
    forward_x(fields[1], send1b)
    to_owners(send1b, recv1b, 3)

    vel_copy.wait()
    lane = lax.broadcasted_iota(jnp.int32, (64, LANES), 1)
    line = lax.broadcasted_iota(jnp.int32, (64, LANES), 0)
    pack_y[0] = vel[:, 63, :]
    pack_y[1] = vel[:, 0, :]

    def pack(b, carry):
        last, first = carry
        value = vel[b]
        last = jnp.where(lane == b, pltpu.roll(value, b + 1, axis=1), last)
        first = jnp.where(lane == b, pltpu.roll(value, b, axis=1), first)
        return last, first

    zero = jnp.zeros((64, LANES), F32)
    last, first = lax.fori_loop(0, 3 * LZ, pack, (zero, zero), unroll=8)
    pack_x[0] = last
    pack_x[1] = first
    up_r, down_r = (row + 1) % ROWS, (row + ROWS - 1) % ROWS
    up_c, down_c = (col + 1) % COLS, (col + COLS - 1) % COLS
    halos = [
        remote(pack_y.at[0], low_y, halo_sems.at[0], halo_sems.at[4], up_r * COLS + col),
        remote(pack_y.at[1], high_y, halo_sems.at[1], halo_sems.at[5], down_r * COLS + col),
        remote(pack_x.at[0], low_x, halo_sems.at[2], halo_sems.at[6], row * COLS + up_c),
        remote(pack_x.at[1], high_x, halo_sems.at[3], halo_sems.at[7], row * COLS + down_c),
    ]
    for h in halos:
        h.start()

    @pl.when(is_owner)
    def _():
        kx, ky, mag, weight = wave_grids(my_p)
        wait_bytes(recv1, recv_sems.at[2])
        re, im = forward_y(recv1)
        spec[0] = re * weight
        spec[1] = im * weight
        inverse_y(spec[0] * mag, spec[1] * mag, send2, 0)
        to_lines(send2, recv2, 4)
        square = mag * mag
        inverse_y(spec[0] * square, spec[1] * square, send2b, 0)
        to_lines(send2b, recv2b, 5)
        inverse_y(-kx * spec[1], kx * spec[0], send2c, 0)
        inverse_y(-ky * spec[1], ky * spec[0], send2c, 1)
        wait_bytes(recv1b, recv_sems.at[3])
        re, im = forward_y(recv1b)
        spec[2] = re * weight
        spec[3] = im * weight
        inverse_y(-kx * spec[3], kx * spec[2], send2c, 2)
        inverse_y(-ky * spec[3], ky * spec[2], send2c, 3)

    wait_bytes(recv2.at[:OWNERS], recv_sems.at[4])
    vert = inverse_x(recv2, 0)
    fields[2] = vert
    forward_x(-fields[1] * vert, send3)
    to_owners(send3, recv3, 7)

    @pl.when(is_owner)
    def _():
        to_lines(send2c, recv2c, 6)
        kx, ky, mag, weight = wave_grids(my_p)
        cube = mag * mag * mag
        inverse_y(spec[0] * cube, spec[1] * cube, send2d, 0)

    wait_bytes(recv2b.at[:OWNERS], recv_sems.at[5])
    fields[3] = inverse_x(recv2b, 0)

    @pl.when(is_owner)
    def _():
        kx, ky, mag, weight = wave_grids(my_p)
        wait_bytes(recv3, recv_sems.at[7])
        re, im = forward_y(recv3)
        factor = weight * mag
        spec[0] = re * factor
        spec[1] = im * factor
        inverse_y(spec[0], spec[1], send4, 0)
        to_lines(send4, recv4, 8)
        inverse_y(spec[0] * mag, spec[1] * mag, send4b, 0)
        to_lines(send4b, recv4b, 9)

    def coarsen(j):
        hi, lo = split(out_t[j])
        spec[4] = dot(hi, pairs_ref[...]) + dot(lo, pairs_ref[...])
        return spec[4, pl.ds(0, 64, stride=2), :] + spec[4, pl.ds(1, 64, stride=2), :]

    wait_bytes(recv2c.at[:OWNERS], recv_sems.at[6])
    for j in range(2):
        slope = inverse_x(recv2c, j)
        fields[5 + j] = slope
        out_t[j] = jnp.transpose(slope)
        coarse_t[j] = coarsen(j)

    def spread_with(send_sem, recv_sem, src, dst):
        for i in (5, 3, 7, 1, 4, 6, 2):
            to = (col + i) % COLS
            remote(src(to), dst, send_sem, recv_sem, row * COLS + to).start()
        pltpu.make_async_copy(src(col), dst, recv_sem).start()

    def spread(k, src, dst):
        spread_with(out_sems.at[k], out_sems.at[6 + k], src, dst)

    def spread_early(k, src, dst):
        spread_with(early_sems.at[k], early_sems.at[3 + k], src, dst)

    few = lambda k: lambda to: coarse_t.at[k, pl.ds(to * 8, 8), :]
    fine = lambda k: lambda to: out_t.at[k, pl.ds(to * LINES, LINES), :]
    my_few, my_fine = pl.ds(col * 8, 8), pl.ds(col * LINES, LINES)
    spread(2, few(0), su_tile.at[my_few, :])
    spread(3, few(1), sv_tile.at[my_few, :])

    wait_bytes(recv4.at[:OWNERS], recv_sems.at[8])
    vert_two = inverse_x(recv4, 0)
    eta = fields[1]
    fields[2] = fields[2] + vert_two
    forward_x(-eta * vert_two - 0.5 * eta * eta * fields[3], send5)
    to_owners(send5, recv5, 10)

    @pl.when(is_owner)
    def _():
        to_lines(send2d, recv2d, 12)

    pot_dx, pot_dy = fields[5], fields[6]
    height_dx, height_dy = inverse_x(recv2c, 2), inverse_x(recv2c, 3)
    stretch = 1.0 + (height_dx * height_dx + height_dy * height_dy)
    advected = -(height_dx * pot_dx + height_dy * pot_dy)
    fields[7] = stretch
    fields[8] = advected
    out_t[0] = jnp.transpose(stretch)
    spread_early(0, fine(0), stretch_out.at[my_fine, :])
    out_t[1] = jnp.transpose(advected)
    spread_early(1, fine(1), advected_out.at[my_fine, :])

    for h in halos:
        h.wait()
    wait_bytes(su_tile, out_sems.at[8])
    wait_bytes(sv_tile, out_sems.at[9])

    def derivs(q, l, top):
        b = q * LZ + l
        mid = vel[b]
        above = jnp.where(l == 0, top, vel[q * LZ + jnp.maximum(l - 1, 0)])
        below = vel[q * LZ + jnp.minimum(l + 1, LZ - 1)]
        east = jnp.where(
            lane == LANES - 1,
            pltpu.roll(high_x[...], LANES - 1 - b, axis=1),
            pltpu.roll(mid, LANES - 1, axis=1),
        )
        west = jnp.where(
            lane == 0,
            pltpu.roll(low_x[...], (LANES - b) % LANES, axis=1),
            pltpu.roll(mid, 1, axis=1),
        )
        north = jnp.where(line == 63, high_y[pl.ds(b, 1), :], pltpu.roll(mid, 63, axis=0))
        south = jnp.where(line == 0, low_y[pl.ds(b, 1), :], pltpu.roll(mid, 1, axis=0))
        lap = east + west + north + south + above + below - 6.0 * mid
        return mid, 0.5 * (east - west), 0.5 * (north - south), 0.5 * (above - below), lap

    def level(l, _):
        depth = jnp.full((64, LANES), l, jnp.int32).astype(F32) + 0.5
        drift_decay = jnp.exp(-2.0 * DECAY_RATE * depth)
        u, u_dx, u_dy, u_dz, u_lap = derivs(0, l, su_tile[...])
        v, v_dx, v_dy, v_dz, v_lap = derivs(1, l, sv_tile[...])
        w, w_dx, w_dy, w_dz, w_lap = derivs(2, l, jnp.zeros((64, LANES), F32))
        vort_x = w_dy - v_dz
        vort_y = u_dz - w_dx
        vort_z = v_dx - u_dy
        drift_u = su_tile[...] * drift_decay
        drift_v = sv_tile[...] * drift_decay

        def advance(mid, dx, dy, dz, lap, force):
            carried = u * dx + v * dy + w * dz
            return mid + FLOW_STEP * (-carried + VISCOSITY * lap + force)

        base[l] = advance(u, u_dx, u_dy, u_dz, u_lap, drift_v * vort_z)
        base[LZ + l] = advance(v, v_dx, v_dy, v_dz, v_lap, -drift_u * vort_z)
        base[2 * LZ + l] = advance(w, w_dx, w_dy, w_dz, w_lap, drift_u * vort_y - drift_v * vort_x)
        return 0

    lax.fori_loop(0, EARLY_LEVELS, level, 0)

    @pl.when(is_owner)
    def _():
        kx, ky, mag, weight = wave_grids(my_p)
        wait_bytes(recv5, recv_sems.at[10])
        re, im = forward_y(recv5)
        factor = weight * mag
        inverse_y(re * factor, im * factor, send6, 0)
        to_lines(send6, recv6, 11)

    eta = fields[1]
    pot_dx, pot_dy = fields[5], fields[6]
    out_t[2] = jnp.transpose(-GRAVITY * eta - 0.5 * (pot_dx * pot_dx + pot_dy * pot_dy))
    spread_early(2, fine(2), still_out.at[my_fine, :])
    lax.fori_loop(EARLY_LEVELS, LZ, level, 0)
    base_copy = pltpu.make_async_copy(base, base_out, load_sems.at[n_tab + 1])
    base_copy.start()
    wait_bytes(recv2d.at[:OWNERS], recv_sems.at[12])
    cube_one = inverse_x(recv2d, 0)
    wait_bytes(recv4b.at[:OWNERS], recv_sems.at[9])
    curve_two = inverse_x(recv4b, 0)
    eta = fields[1]
    fields[2] = fields[2] + eta * (fields[3] + curve_two) + 0.5 * eta * eta * cube_one

    out_t[4] = jnp.transpose(eta)
    coarse_t[3] = coarsen(4)

    wait_bytes(recv6.at[:OWNERS], recv_sems.at[11])
    height_rate = fields[8] + fields[7] * (fields[2] + inverse_x(recv6, 0))
    out_t[3] = jnp.transpose(height_rate)
    spread(0, fine(3), height_out.at[my_fine, :])
    pressure = GRAVITY * (coarse_t[3] + SURFACE_STEP * coarsen(3))
    coarse_t[2] = pressure
    spread(5, few(2), press_out.at[pl.ds(col * 8 + 8, 8), :])

    @pl.when(col == COLS - 1)
    def _():
        for to in range(COLS):
            remote(
                coarse_t.at[2, pl.ds(to * 8, 8), :],
                press_out.at[pl.ds(0, 8), :],
                out_sems.at[12],
                out_sems.at[11],
                up_r * COLS + to,
            ).start()

    @pl.when(col == 0)
    def _():
        for to in range(COLS):
            remote(
                coarse_t.at[2, pl.ds(to * 8, 8), :],
                press_out.at[pl.ds(72, 8), :],
                out_sems.at[12],
                out_sems.at[11],
                down_r * COLS + to,
            ).start()

    east = pltpu.roll(pressure, LANES - 1, axis=1)
    east = jnp.where(lane == LANES - 1, pltpu.roll(east, 56, axis=0), east)
    west = pltpu.roll(pressure, 1, axis=1)
    west = jnp.where(lane == 0, pltpu.roll(west, 8, axis=0), west)
    coarse_t[3] = 0.5 * (east - west)
    spread(4, few(3), lx_out.at[my_few, :])

    for f in range(2):
        wait_bytes(lines.at[f, :7], send_sems.at[f])
    wait_bytes(out_t.at[3, :112, :], out_sems.at[0])
    for k in range(3):
        wait_bytes(out_t.at[k, :112, :], early_sems.at[k])
    for k in range(4):
        wait_bytes(coarse_t.at[k, :56, :], out_sems.at[2 + k])

    @pl.when((col == 0) | (col == COLS - 1))
    def _():
        wait_bytes(coarse_t.at[2], out_sems.at[12])

    owned = ((send1, 2), (send1b, 3), (send3, 7), (send5, 10))

    @pl.when(is_owner)
    def _():
        for buf, k in owned:
            wait_bytes(buf.at[: OWNERS - 1], send_sems.at[k])
        for buf, k in (
            (send2, 4),
            (send2b, 5),
            (send2c, 6),
            (send2d, 12),
            (send4, 8),
            (send4b, 9),
            (send6, 11),
        ):
            wait_bytes(buf.at[: DEVS - 1], send_sems.at[k])

    @pl.when(jnp.logical_not(is_owner))
    def _():
        for buf, k in owned:
            wait_bytes(buf.at[:OWNERS], send_sems.at[k])

    base_copy.wait()
    for k, ref in enumerate((stretch_out, advected_out, still_out)):
        wait_bytes(ref, early_sems.at[3 + k])
    for k, ref in ((0, height_out), (4, lx_out), (5, press_out)):
        wait_bytes(ref, out_sems.at[6 + k])


CHUNK = 8


def load_kernel(*refs):
    load_x, press, height, stretch, advected, still, base = refs[:7]
    out, height_out, pot_out = refs[7:10]
    stage, pot, sems = refs[10:]
    straight = [
        pltpu.make_async_copy(height, height_out, sems.at[0]),
        pltpu.make_async_copy(base.at[pl.ds(2 * LZ, LZ)], out.at[pl.ds(2 * LZ, LZ)], sems.at[1]),
    ]
    for copy in straight:
        copy.start()
    loads = (load_x[...], 0.5 * (press[9:73, :] - press[7:71, :]))
    outs = []
    for k in range(2 * LZ // CHUNK):
        for b in range(CHUNK * k, CHUNK * k + CHUNK):
            q, l = divmod(b, LZ)
            decay = float(np.exp(-DECAY_RATE * (l + 0.5)))
            stage[b] = base[b] - (FLOW_STEP * decay) * loads[q]
        part = pl.ds(CHUNK * k, CHUNK)
        outs.append(pltpu.make_async_copy(stage.at[part], out.at[part], sems.at[3 + k]))
        outs[-1].start()
    lifted = height[...] - advected[...]
    pot[...] = still[...] + 0.5 * lifted * (lifted / stretch[...])
    outs.append(pltpu.make_async_copy(pot, pot_out, sems.at[2]))
    outs[-1].start()
    for copy in straight + outs:
        copy.wait()


def in_hbm(a):
    return pltpu.with_memory_space_constraint(a, pltpu.HBM)


def local(surface_height, surface_potential, velocity):
    flow = velocity.reshape(3 * LZ, 64, LANES)
    tabs = [jnp.asarray(t) for t in tables()]
    anywhere = pl.BlockSpec(memory_space=pl.ANY)

    def shape(*dims):
        return jax.ShapeDtypeStruct(dims, F32)

    def buf(*dims):
        return VMEM(dims, F32)

    messages = []
    for kind, count in zip("oollllollol", (2, 2, 2, 2, 8, 2, 2, 2, 2, 2, 2)):
        if kind == "o":
            messages += [buf(OWN_PAD, count, LANES), buf(DEVS, count, LANES)]
        else:
            messages += [buf(DEVS, count, LANES), buf(OWN_PAD, count, LANES)]
    outs = pl.pallas_call(
        surface_kernel,
        name="surface",
        out_shape=[
            shape(128, 256),
            shape(64, LANES),
            shape(80, LANES),
            shape(3 * LZ, 64, LANES),
            shape(128, 256),
            shape(128, 256),
            shape(128, 256),
        ],
        in_specs=[anywhere] * (3 + len(tabs)),
        out_specs=[anywhere] * 7,
        scratch_shapes=[VMEM(t.shape, t.dtype) for t in tabs]
        + [buf(2, COLS, LINES, 256), buf(9, 256, LANES)]
        + messages
        + [
            buf(5, LANES, LANES),
            buf(5, LANES, 256),
            buf(4, 64, LANES),
            buf(3 * LZ, 64, LANES),
            buf(3 * LZ, 64, LANES),
            buf(2, 48, LANES),
            buf(2, 64, LANES),
            buf(48, LANES),
            buf(48, LANES),
            buf(64, LANES),
            buf(64, LANES),
            buf(64, LANES),
            buf(64, LANES),
            pltpu.SMEM((DEVS,), jnp.int32),
            pltpu.SMEM((DEVS,), jnp.int32),
            pltpu.SMEM((DEVS,), jnp.int32),
            pltpu.SemaphoreType.DMA((len(tabs) + 2,)),
            pltpu.SemaphoreType.DMA((13,)),
            pltpu.SemaphoreType.DMA((13,)),
            pltpu.SemaphoreType.DMA((13,)),
            pltpu.SemaphoreType.DMA((6,)),
            pltpu.SemaphoreType.DMA((8,)),
        ],
        compiler_params=pltpu.CompilerParams(
            collective_id=0, has_side_effects=True, vmem_limit_bytes=SURFACE_VMEM
        ),
    )(*(in_hbm(a) for a in (surface_potential, surface_height, flow, *tabs)))
    height_rate, lx, press, base, stretch, advected, still = outs
    nxt, height_rate, potential_rate = pl.pallas_call(
        load_kernel,
        name="load",
        out_shape=[shape(3 * LZ, 64, LANES), shape(128, 256), shape(128, 256)],
        in_specs=[pl.BlockSpec(memory_space=VMEM)] * 7,
        out_specs=[anywhere] * 3,
        scratch_shapes=[
            buf(2 * LZ, 64, LANES),
            buf(128, 256),
            pltpu.SemaphoreType.DMA((3 + 2 * LZ // CHUNK,)),
        ],
        compiler_params=pltpu.CompilerParams(vmem_limit_bytes=LOAD_VMEM),
    )(lx, press, height_rate, stretch, advected, still, base)
    return height_rate, potential_rate, nxt.reshape(velocity.shape)


def solution(mesh):
    specs = (P("row", "col"), P("row", "col"), P(None, None, "row", "col"))
    return jax.shard_map(local, mesh=mesh, in_specs=specs, out_specs=specs, check_vma=False)
```
